128 devices in a mesh: seq: 8 (over z, core), tp: 16 (over x, y).
Axes of the slice: x: 4, y: 4, z: 4, core: 2. Of those that a mesh axis runs over, the one named last changes fastest.
Arguments:
- patches: bfloat16 [32768, 1280], P(('seq', 'tp')), may hold values from -6 to 6
- image_table: int32 [256, 3], replicated, may hold values from 0 to 4095, as said below
- ln_gain: float32 [1280], replicated, may hold values from 0.25 to 1.75
- ln_bias: float32 [1280], replicated, may hold values from -3 to 3
- merge_up: bfloat16 [5120, 5120], P(None, 'tp'), may hold values from -0.078125 to 0.078125
- merge_up_bias: float32 [5120], P('tp'), may hold values from -3 to 3
- merge_down: bfloat16 [5120, 3584], P('tp'), may hold values from -0.15625 to 0.15625
- merge_down_bias: float32 [3584], replicated, may hold values from -3 to 3
- text_embeds: bfloat16 [4096, 3584], P('seq', 'tp'), may hold values from -6 to 6
- attn_gain: float32 [3584], replicated, may hold values from 0.25 to 1.75
- q_weight: bfloat16 [3584, 2048], P(None, 'tp'), may hold values from -2 to 2
- q_bias: float32 [2048], P('tp'), may hold values from -3 to 3
- key_value_weight: bfloat16 [3584, 1024], replicated, may hold values from -2 to 2
- key_value_bias: float32 [1024], replicated, may hold values from -3 to 3
- o_weight: bfloat16 [2048, 3584], P('tp'), may hold values from -0.1875 to 0.1875
Outputs:
- block_out: bfloat16 [4096, 3584], P('seq', 'tp')
The draws below stay inside these ranges and needn't reach their ends.
Inputs may be any that keep to these rules, and one draw needn't show every extreme that they name: `image_table`: grid entries are even. Table rows 2d and 2d + 1 are the two images of device d = seq index * 16 + tp index; the second starts right after the first, so the device's tokens fill consecutive positions inside block [s * 512, (s + 1) * 512) of its seq index s. Images never intersect. The two images of a device hold at most 64 merged tokens, and in every seq group one device holds exactly 64. A sequence block holds at most 424 image tokens, and some block holds exactly that many.
All inputs are finite; a program needn't handle non-finite values.
Results may differ from the reference program's by a relative error of at most 0.012.
Values may be sent and summed in bfloat16 or wider, within the bound.
A program may use at most 128 MiB of HBM per device.

```python
import jax
import jax.numpy as jnp
from jax import lax

MODEL_WIDTH = 3584
VW = 1280
HEAD_DIMENSION = 128
KEY_VALUE_HEADS = 4
LOCAL_QUERY_HEAD = 16
CAP = 64
TOK_SEQ = 512
MW = 5120
PACKED_LENGTH = 4096
N_SEQ = 8
N_TP = 16
DEVICES = 128


def table_parts(key):
    groups = N_SEQ
    members = N_TP
    heights = jax.random.randint(jax.random.fold_in(key, 101), (groups, members, 2), 2, 5)
    widths = jax.random.randint(jax.random.fold_in(key, 102), (groups, members, 2), 2, 4)
    fullest = jax.random.randint(jax.random.fold_in(key, 108), (), 0, groups)
    is_fullest = (jnp.arange(groups) == fullest)[:, None, None]
    heights = jnp.where(is_fullest, 4, heights)
    widths = jnp.where(is_fullest, 3, widths)
    largest = jax.random.randint(jax.random.fold_in(key, 103), (groups,), 0, members)
    large_width = 2 ** jax.random.randint(jax.random.fold_in(key, 104), (groups,), 1, 4)
    large_rows = CAP // large_width
    first_rows = jax.random.randint(jax.random.fold_in(key, 105), (groups,), 1, large_rows)
    large_heights = jnp.stack([first_rows, large_rows - first_rows], axis=1)
    is_large = jnp.arange(members)[None, :] == largest[:, None]
    heights = jnp.where(is_large[:, :, None], large_heights[:, None, :], heights)
    widths = jnp.where(is_large[:, :, None], large_width[:, None, None], widths)
    counts = heights * widths
    run_sizes = jnp.sum(counts, axis=2)
    orders = jax.vmap(lambda inner_key: jax.random.permutation(inner_key, members))(jax.random.split(jax.random.fold_in(key, 106), groups))
    ordered_sizes = jnp.take_along_axis(run_sizes, orders, axis=1)
    spare = TOK_SEQ - jnp.sum(run_sizes, axis=1)
    cuts = jnp.sort(jax.random.randint(jax.random.fold_in(key, 107), (groups, members), 0, spare[:, None] + 1), axis=1)
    before = jnp.cumsum(ordered_sizes, axis=1) - ordered_sizes
    ordered_starts = jnp.arange(groups)[:, None] * TOK_SEQ + cuts + before
    run_starts = jnp.zeros((groups, members), jnp.int32).at[jnp.arange(groups)[:, None], orders].set(ordered_starts.astype(jnp.int32))
    offsets = jnp.stack([run_starts, run_starts + counts[:, :, 0]], axis=-1)
    table = jnp.stack([2 * heights, 2 * widths, offsets], axis=-1)
    return table.reshape(groups * members * 2, 3).astype(jnp.int32)


def draw_image_table(key, part):
    return table_parts(key)


def draw_text_embeds(key, part):
    row_data = jax.random.normal(jax.random.fold_in(key, 53), (PACKED_LENGTH, MODEL_WIDTH), jnp.float32)
    return jnp.clip(row_data, -6.0, 6.0).astype(jnp.bfloat16)


def columns_of_key(key):
    return jax.random.normal(jax.random.fold_in(key, 31), (MODEL_WIDTH, 2 * KEY_VALUE_HEADS * HEAD_DIMENSION), jnp.float32) * MODEL_WIDTH ** (-0.5)


def draw_key_value_weight(key, part):
    return jnp.clip(columns_of_key(key), -2.0, 2.0).astype(jnp.bfloat16)


def draw_q_weight(key, part):
    base = jax.random.normal(jax.random.fold_in(key, 37), (MODEL_WIDTH, LOCAL_QUERY_HEAD * HEAD_DIMENSION), jnp.float32) * MODEL_WIDTH ** (-0.5)
    return jnp.clip(base, -2.0, 2.0).astype(jnp.bfloat16)


def spiked(result, own_key, source, target, blocks, factor):
    def block_of(position):
        return (jnp.arange(result.shape[position]) // (result.shape[position] // blocks)).reshape((-1,) + (1,) * (result.ndim - 1 - position))

    one_side = jax.random.permutation(own_key, blocks)[block_of(target)]
    other_side = (block_of(target) + blocks // 2) % blocks
    return jnp.where((block_of(source) == one_side) | (block_of(source) == other_side), factor * result, result)


def levels(own_key, extent, shards, low, top_value):
    level = 1.0
    for axis_at, shards_of in shards:
        draws = jax.random.uniform(jax.random.fold_in(jax.random.fold_in(own_key, 6), axis_at), (shards_of,), jnp.float32, low / len(shards), top_value / len(shards))
        level = level * jnp.repeat(jnp.exp(draws), extent[axis_at] // shards_of).reshape((-1,) + (1,) * (len(extent) - 1 - axis_at))
    return level


def bell_draw(key, dims, scale, reach, cuts=(), held_as=jnp.bfloat16):
    factor_of = levels(key, dims, cuts, -0.22, 0.18) if cuts else 1.0
    result = jax.random.normal(key, dims, jnp.float32) * scale * factor_of
    return jnp.minimum(jnp.maximum(result, -reach), reach).astype(held_as)


def bell_draw_with(own_key, shape, scale, most, shards, heavy, kind=jnp.bfloat16):
    entries = scale * jax.random.normal(own_key, shape, jnp.float32)
    if shards:
        entries = entries * levels(own_key, shape, shards, -0.22, 0.18)
    return jnp.clip(spiked(entries, jax.random.fold_in(own_key, 3), *heavy), -most, most).astype(kind)


def setup_inputs(seed: int = 0) -> dict:
    keys = jax.random.split(jax.random.key(seed), 16)
    return {
        "patches": bell_draw(keys[0], (4 * CAP * DEVICES, VW), 1.0, 6.0, ((0, 128),)),
        "image_table": draw_image_table(jax.random.fold_in(keys[15], 71), 0),
        "ln_gain": jnp.clip(1.0 + 0.15 * jax.random.normal(keys[2], (VW,), jnp.float32), 0.25, 1.75),
        "ln_bias": bell_draw(keys[3], (VW,), 0.5, 3.0, (), jnp.float32),
        "merge_up": bell_draw(keys[4], (MW, MW), MW ** -0.5, 0.078125, ((1, 16),)),
        "merge_up_bias": bell_draw(keys[5], (MW,), 0.5, 3.0, ((0, 16),), jnp.float32),
        "merge_down": bell_draw_with(keys[6], (MW, MODEL_WIDTH), (MW // 2) ** -0.5, 0.15625, ((0, 16),), (0, 1, 16, 2.0)),
        "merge_down_bias": bell_draw(keys[7], (MODEL_WIDTH,), 0.5, 3.0, (), jnp.float32),
        "text_embeds": draw_text_embeds(jax.random.fold_in(keys[15], 71), 0),
        "attn_gain": jnp.clip(1.0 + 0.15 * jax.random.normal(keys[9], (MODEL_WIDTH,), jnp.float32), 0.25, 1.75),
        "q_weight": draw_q_weight(jax.random.fold_in(keys[15], 71), 0),
        "q_bias": bell_draw(keys[11], (LOCAL_QUERY_HEAD * HEAD_DIMENSION,), 0.5, 3.0, ((0, 16),), jnp.float32),
        "key_value_weight": draw_key_value_weight(jax.random.fold_in(keys[15], 71), 0),
        "key_value_bias": bell_draw(keys[13], (2 * KEY_VALUE_HEADS * HEAD_DIMENSION,), 0.5, 3.0, (), jnp.float32),
        "o_weight": bell_draw_with(keys[14], (LOCAL_QUERY_HEAD * HEAD_DIMENSION, MODEL_WIDTH), (LOCAL_QUERY_HEAD * HEAD_DIMENSION) ** -0.5, 0.1875, ((0, 16),), (0, 1, 16, 2.0)),
    }


EPS = 1e-06
THETA = 1000000.0

def layer_norm(row_data, scale_row, offset_row):
    centre = lax.optimization_barrier(jnp.mean(row_data, axis=-1, keepdims=True))
    centred = row_data - centre
    spread = lax.optimization_barrier(jnp.mean(centred * centred, axis=-1, keepdims=True))
    return centred * lax.rsqrt(spread + EPS) * scale_row + offset_row

def image_fields(image_table):
    grid_h = image_table[:, 0]
    grid_w = image_table[:, 1]
    across = grid_w // 2
    return (across, grid_h // 2 * across, image_table[:, 2])

def rope_tables(positions, image_table, head_size):
    across, counts, offsets = image_fields(image_table)
    inside = ((positions[:, None] >= offsets[None, :]) & (positions[:, None] < (offsets + counts)[None, :])).astype(jnp.int32)
    is_image = lax.optimization_barrier(jnp.sum(inside, axis=1))
    run_start = lax.optimization_barrier(jnp.sum(inside * offsets[None, :], axis=1))
    row_width = lax.optimization_barrier(jnp.sum(inside * across[None, :], axis=1)) + (1 - is_image)
    inner_index = positions - run_start
    pos_t = jnp.where(is_image > 0, run_start, positions)
    pos_h = jnp.where(is_image > 0, run_start + inner_index // row_width, positions)
    pos_w = jnp.where(is_image > 0, run_start + inner_index % row_width, positions)
    half_size = head_size // 2
    frequency = jnp.arange(half_size, dtype=jnp.int32)
    inverse = THETA ** (-2.0 * frequency.astype(jnp.float32) / head_size)
    first_cut = head_size // 8
    second_cut = first_cut + 3 * head_size // 16
    chosen = jnp.where(frequency[None, :] < first_cut, pos_t[:, None], jnp.where(frequency[None, :] < second_cut, pos_h[:, None], pos_w[:, None]))
    angles = chosen.astype(jnp.float32) * inverse[None, :]
    angles = jnp.concatenate([angles, angles], axis=1)
    return (jnp.cos(angles), jnp.sin(angles), is_image)

def apply_rotation(value_tensor, cosine_values, sine_lookup):
    half_size = value_tensor.shape[-1] // 2
    turned = jnp.concatenate([-value_tensor[..., half_size:], value_tensor[..., :half_size]], axis=-1)
    return value_tensor * cosine_values[:, None, :] + turned * sine_lookup[:, None, :]

def reference(patches, image_table, ln_gain, ln_bias, merge_up, merge_up_bias, merge_down, merge_down_bias, text_embeds, attn_gain, q_weight, q_bias, key_value_weight, key_value_bias, o_weight):
    normed = layer_norm(patches.astype(jnp.float32), ln_gain, ln_bias).astype(jnp.bfloat16)
    merged = normed.reshape(-1, MW)
    positions = jnp.arange(PACKED_LENGTH, dtype=jnp.int32)
    cosine_values, sine_lookup, is_image = rope_tables(positions, image_table, HEAD_DIMENSION)
    across, counts, offsets = image_fields(image_table)
    covered = ((positions[:, None] >= offsets[None, :]) & (positions[:, None] < (offsets + counts)[None, :])).astype(jnp.int32)
    image_number = lax.optimization_barrier(jnp.sum(covered * jnp.arange(offsets.shape[0], dtype=jnp.int32)[None, :], axis=1))
    device_number = image_number // 2
    run_start = jnp.take(offsets, 2 * device_number)
    picked = jnp.where(is_image > 0, device_number * CAP + positions - run_start, 0).astype(jnp.int32)
    vision = jnp.take(merged, picked, axis=0) * is_image[:, None].astype(jnp.bfloat16)
    image_weight = is_image.astype(jnp.float32)
    lifted = jnp.dot(vision, merge_up, preferred_element_type=jnp.float32) + merge_up_bias
    hidden = (jax.nn.gelu(lifted, approximate=False) * image_weight[:, None]).astype(jnp.bfloat16)
    projected = jnp.dot(hidden, merge_down, preferred_element_type=jnp.float32) + merge_down_bias
    residual = jnp.where(is_image[:, None] > 0, projected, text_embeds.astype(jnp.float32))
    scale_rows = lax.rsqrt(lax.optimization_barrier(jnp.mean(residual * residual, axis=1)) + EPS)
    normed_rows = (residual * scale_rows[:, None] * attn_gain[None, :]).astype(jnp.bfloat16)
    query = jnp.dot(normed_rows, q_weight, preferred_element_type=jnp.float32) + q_bias
    query = apply_rotation(query.reshape(PACKED_LENGTH, LOCAL_QUERY_HEAD, HEAD_DIMENSION), cosine_values, sine_lookup).astype(jnp.bfloat16)
    projected_key_value = jnp.dot(normed_rows, key_value_weight, preferred_element_type=jnp.float32) + key_value_bias
    key_tensor = apply_rotation(projected_key_value[:, :KEY_VALUE_HEADS * HEAD_DIMENSION].reshape(PACKED_LENGTH, KEY_VALUE_HEADS, HEAD_DIMENSION), cosine_values, sine_lookup).astype(jnp.bfloat16)
    value_tensor = projected_key_value[:, KEY_VALUE_HEADS * HEAD_DIMENSION:].reshape(PACKED_LENGTH, KEY_VALUE_HEADS, HEAD_DIMENSION).astype(jnp.bfloat16)
    query_heads = query.transpose(1, 0, 2)
    key_heads = key_tensor.transpose(1, 0, 2)
    value_heads = value_tensor.transpose(1, 0, 2)
    heads_per_group = LOCAL_QUERY_HEAD // KEY_VALUE_HEADS
    allowed = positions[None, :] <= positions[:, None]

    def one_head(head_index):
        query_head = query_heads[head_index]
        single_key_head = key_heads[head_index // heads_per_group]
        value_head = value_heads[head_index // heads_per_group]
        scores = jnp.dot(query_head, single_key_head.T, preferred_element_type=jnp.float32) * HEAD_DIMENSION ** (-0.5)
        scores = jnp.where(allowed, scores, -1e+30)
        top_score = lax.optimization_barrier(jnp.max(scores, axis=1))
        weights = jnp.where(allowed, jnp.exp(scores - top_score[:, None]), 0.0)
        summed = jnp.dot(weights.astype(jnp.bfloat16), value_head, preferred_element_type=jnp.float32)
        return (summed / lax.optimization_barrier(jnp.sum(weights, axis=1))[:, None]).astype(jnp.bfloat16)
    attention = lax.map(one_head, jnp.arange(LOCAL_QUERY_HEAD, dtype=jnp.int32))
    attention = attention.transpose(1, 0, 2).reshape(PACKED_LENGTH, LOCAL_QUERY_HEAD * HEAD_DIMENSION)
    output_rows = residual + jnp.dot(attention, o_weight, preferred_element_type=jnp.float32)
    return output_rows.astype(jnp.bfloat16)
```

```python
import functools

import jax
import jax.numpy as jnp
from jax import lax
from jax.experimental import pallas as pl
from jax.experimental.pallas import tpu as pltpu
from jax.sharding import PartitionSpec as P

MESH = pl.DeviceIdType.MESH
HEAD_DIMENSION = 128
KEY_VALUE_HEADS = 4
LOCAL_QUERY_HEAD = 16
CAP = 64
TOK_SEQ = 512
MW = 5120
VW = 1280
WIDTH = 3584
HID = 320
COLS = 224
N_TP = 16
N_SEQ = 8
SIDE = 4
ROWS = 448
HALF = 112
TCOL = 640
BLK = 896
RB = 128

EPS = 1e-06
THETA = 1000000.0
F32 = jnp.float32
BF16 = jnp.bfloat16


def al(value, multiple):
    return pl.multiple_of(value, multiple)


def place():
    t = lax.axis_index("tp")
    return t, t // SIDE, lax.rem(t, SIDE)


def wrap(value):
    return lax.rem(value + 2 * SIDE, SIDE)


def at_xy(x, y):
    return wrap(x) * SIDE + wrap(y)


def offset_xy(half, i, j):
    t, x, y = place()
    return (wrap(x + j), wrap(y + i)) if half == 0 else (wrap(x + i), wrap(y + j))


def peer(half, phase, sign):
    x, y = offset_xy(half, sign, 0) if phase == 1 else offset_xy(half, 0, sign)
    return x * SIDE + y


class Link:
    def __init__(self, send_sem, recv_sem, axis="tp"):
        self.send_sem, self.recv_sem, self.axis = send_sem, recv_sem, axis
        self.number, self.open = {}, []

    def _copy(self, key, src, dst, device):
        k = self.number.setdefault(key, len(self.number))
        return pltpu.make_async_remote_copy(
            src_ref=src,
            dst_ref=dst,
            send_sem=self.send_sem.at[k],
            recv_sem=self.recv_sem.at[k],
            device_id={self.axis: device},
            device_id_type=MESH,
        )

    def send(self, key, src, dst, device):
        copy = self._copy(key, src, dst, device)
        copy.start()
        self.open.append(copy)

    def arrived(self, key, dst, device):
        self._copy(key, dst, dst, device).wait_recv()

    def drain(self):
        assert len(self.number) <= self.send_sem.shape[0]
        for copy in self.open:
            copy.wait_send()
        self.open = []


def greet(devices, axis="tp"):
    barrier = pltpu.get_barrier_semaphore()
    for device in devices:
        pl.semaphore_signal(barrier, inc=1, device_id={axis: device}, device_id_type=MESH)
    pl.semaphore_wait(barrier, len(devices))


def ring_peers():
    return [peer(0, 1, 1), peer(0, 1, -1), peer(0, 2, 1), peer(0, 2, -1)]


def all_gather_2d(link, region):
    def reg(half, i, j, part):
        x, y = offset_xy(half, i, j)
        return region(half, x, y, part)

    def send(key, half, phase, sign, i, j, part):
        ref = reg(half, i, j, part)
        link.send((half, *key), ref, ref, peer(half, phase, sign))

    def got(key, half, phase, sign, i, j, part):
        link.arrived((half, *key), reg(half, i, j, part), peer(half, phase, -sign))

    both = ((1, 0), (-1, 1))
    halves = (0, 1)
    for h in halves:
        for s, _ in both:
            send(("p1", s), h, 1, s, 0, 0, None)
    for h in halves:
        for s, _ in both:
            send(("p2", s, 0), h, 2, s, 0, 0, None)
    for s, part in both:
        for h in halves:
            got(("p1", s), h, 1, s, -s, 0, None)
            send(("r1", s), h, 1, s, -s, 0, part)
            for s2, _ in both:
                send(("p2", s2, -s), h, 2, s2, -s, 0, None)
    for s, part in both:
        for h in halves:
            got(("p2", s, 0), h, 2, s, 0, -s, None)
            send(("r2", s, 0), h, 2, s, 0, -s, part)
    for s, part in both:
        for h in halves:
            got(("r1", s), h, 1, s, 2, 0, part)
            for s2, _ in both:
                send(("p2", s2, 2, part), h, 2, s2, 2, 0, part)
    for i in (-1, 1):
        for s, part in both:
            for h in halves:
                got(("p2", s, i), h, 2, s, i, -s, None)
                send(("r2", s, i), h, 2, s, i, -s, part)
    for s, part in both:
        for h in halves:
            got(("p2", s, 2, part), h, 2, s, 2, -s, part)
            send(("r2", s, 2), h, 2, s, 2, -s, part)
    for s, part in both:
        for h in halves:
            got(("p2", s, 2, 1 - part), h, 2, s, 2, -s, 1 - part)
    for i in (0, -1, 1, 2):
        for s, part in both:
            for h in halves:
                got(("r2", s, i), h, 2, s, i, 2, part)


AG_SEMS = 44


def tokens_kernel(patches, gain, bias, src_row, target, out, outgoing, incoming, send_sem, recv_sem):
    t, x, y = place()
    greet([lax.rem(t + o, N_TP) for o in range(1, N_TP)])
    link = Link(send_sem, recv_sem)
    rows = patches[...].astype(F32)
    centre = jnp.mean(rows, axis=-1, keepdims=True)
    centred = rows - centre
    spread = jnp.mean(centred * centred, axis=-1, keepdims=True)
    normed = (centred * lax.rsqrt(spread + EPS) * gain[...] + bias[...]).astype(BF16)
    lane = lax.broadcasted_iota(jnp.int32, (CAP, 4 * CAP), 1)
    for q in range(4):
        pick = (lane == src_row[...] + q).astype(BF16)
        part = jnp.dot(pick, normed, preferred_element_type=F32).astype(BF16)
        for u in range(2):
            for r in range(2):
                outgoing[2 * (2 * q + u) + r] = part[r * 32 : (r + 1) * 32, u * TCOL : (u + 1) * TCOL]
    for o in range(1, N_TP):
        to = lax.rem(t + o, N_TP)
        link.send(("a", o), outgoing.at[to], incoming.at[t], to)
    incoming[t] = outgoing[t]
    for o in range(1, N_TP):
        frm = lax.rem(t - o + N_TP, N_TP)
        link.arrived(("a", o), incoming.at[frm], frm)
    slots = incoming[...].reshape(N_TP * 32, TCOL)
    pick = (lax.broadcasted_iota(jnp.int32, (2 * HALF, N_TP * 32), 0) == target[...]).astype(BF16)
    mine = jnp.dot(pick, slots, preferred_element_type=F32).astype(BF16)
    out[pl.ds(al(lax.rem(t, 2) * 2 * HALF, 2 * HALF), 2 * HALF), pl.ds(al(t // 2 * TCOL, 128), TCOL)] = mine

    def region(half, x, y, part):
        d = x * SIDE + y
        first, width = ((0, TCOL), (0, 384), (384, 256))[0 if part is None else 1 + part]
        return out.at[
            pl.ds(al(lax.rem(d, 2) * 2 * HALF + half * HALF, 16), HALF),
            pl.ds(al(d // 2 * TCOL + first, 128), width),
        ]

    all_gather_2d(link, region)
    link.drain()


def gather_tokens(patches, gain, bias, src_row, target):
    vmem = pl.BlockSpec(memory_space=pltpu.VMEM)
    return pl.pallas_call(
        tokens_kernel,
        out_shape=jax.ShapeDtypeStruct((ROWS, MW), BF16),
        in_specs=[vmem] * 5,
        out_specs=vmem,
        scratch_shapes=[
            pltpu.VMEM((N_TP, 32, TCOL), BF16),
            pltpu.VMEM((N_TP, 32, TCOL), BF16),
            pltpu.SemaphoreType.DMA((AG_SEMS + N_TP,)),
            pltpu.SemaphoreType.DMA((AG_SEMS + N_TP,)),
        ],
        compiler_params=pltpu.CompilerParams(collective_id=0, has_side_effects=True),
        name="tokens",
    )(patches, gain, bias, src_row, target)


def merger_kernel(
    tokens, up, up_bias, src, down, text, out,
    lifted, hidden, part_ref,
    a_raw, a_mid, a_out, a_sum, b_raw, b_mid, b_out, b_sum,
    c_raw, c_mid, c_out, send_sem, recv_sem,
):
    t, x, y = place()
    greet(ring_peers())
    link = Link(send_sem, recv_sem)
    lifted[...] = jnp.zeros_like(lifted)

    def lift(k, carry):
        cols = pl.ds(al(k * TCOL, 128), TCOL)
        lifted[...] += jnp.dot(tokens[:, cols], up[cols, :], preferred_element_type=F32)
        return carry

    lax.fori_loop(0, MW // TCOL, lift, 0)
    raised = lifted[...] + up_bias[...]
    act = (0.5 * raised * (1.0 + lax.erf(raised * 0.5**0.5))).astype(BF16)
    pick = (lax.broadcasted_iota(jnp.int32, (TOK_SEQ, ROWS), 1) == src[...]).astype(BF16)
    hidden[...] = jnp.dot(pick, act, preferred_element_type=F32).astype(BF16)

    def lower(i, carry):
        for rb in range(SIDE):
            got = jnp.dot(hidden[rb * RB : (rb + 1) * RB, :], down[:, pl.ds(al(i * BLK, 128), BLK)], preferred_element_type=F32)
            part_ref[rb, :, pl.ds(al(i * BLK, 128), BLK)] = got.astype(BF16)
        return carry

    lax.fori_loop(0, SIDE, lower, 0)
    spot = (
        lax.broadcasted_iota(jnp.int32, (COLS, BLK), 0) + y * COLS == lax.broadcasted_iota(jnp.int32, (COLS, BLK), 1)
    ).astype(BF16)
    own = pl.ds(al(x * BLK, 128), BLK)
    for rb in range(SIDE):
        add = jnp.dot(text[rb * RB : (rb + 1) * RB, :], spot, preferred_element_type=F32)
        part_ref[rb, :, own] = (part_ref[rb, :, own].astype(F32) + add).astype(BF16)
    half_rows = RB // 2

    def a_piece(i, part):
        rows = (pl.ds(0, SIDE), pl.ds(0, 2), pl.ds(2, 2))[0 if part is None else 1 + part]
        return part_ref.at[rows, pl.ds(0, half_rows), pl.ds(al(wrap(x + i) * BLK, 128), BLK)]

    def b_piece(i, part):
        cols = (pl.ds(0, WIDTH), pl.ds(0, WIDTH // 2), pl.ds(WIDTH // 2, WIDTH // 2))[0 if part is None else 1 + part]
        return part_ref.at[wrap(y + i), pl.ds(half_rows, half_rows), cols]

    def to_x(s):
        return at_xy(x + s, y)

    def to_y(s):
        return at_xy(x, y + s)

    def mid_of(ref, name, part):
        if name == "a":
            return ref.at[pl.ds(2 * part, 2)]
        return ref.at[:, pl.ds(part * (WIDTH // 2), WIDTH // 2)]

    sides = (("a", a_piece, a_raw, a_mid, a_out, to_x), ("b", b_piece, b_raw, b_mid, b_out, to_y))
    signs = ((1, 0), (-1, 1))
    for n, piece, raw, mid, outb, to in sides:
        for s, part in signs:
            link.send((n, "raw", s), piece(2, part), raw.at[part], to(s))
    for n, piece, raw, mid, outb, to in sides:
        for s, part in signs:
            link.send((n, "own", s), piece(s, 1 - part), mid_of(mid.at[part], n, 1 - part), to(s))
    for n, piece, raw, mid, outb, to in sides:
        for s, part in signs:
            link.arrived((n, "raw", s), raw.at[part], to(-s))
            outb[part] = (raw[part].astype(F32) + piece(s, part)[...].astype(F32)).astype(BF16)
            link.send((n, "sum", s), outb.at[part], mid_of(mid.at[part], n, part), to(s))
    for n, piece, raw, mid, outb, to in sides:
        for s, part in signs:
            link.arrived((n, "own", s), mid_of(mid.at[part], n, 1 - part), to(-s))
            link.arrived((n, "sum", s), mid_of(mid.at[part], n, part), to(-s))
    a_sum[...] = (a_piece(0, None)[...].astype(F32) + a_mid[0].astype(F32) + a_mid[1].astype(F32)).astype(BF16)
    b_sum[...] = (b_piece(0, None)[...].astype(F32) + b_mid[0].astype(F32) + b_mid[1].astype(F32)).astype(BF16)

    quarter = half_rows // 2

    def a_next(i, part):
        rows = (pl.ds(0, half_rows), pl.ds(0, quarter), pl.ds(quarter, quarter))[0 if part is None else 1 + part]
        return a_sum.at[wrap(y + i), rows, :]

    def b_next(i, part):
        rows = (pl.ds(0, half_rows), pl.ds(0, quarter), pl.ds(quarter, quarter))[0 if part is None else 1 + part]
        return b_sum.at[rows, pl.ds(al(wrap(x + i) * BLK, 128), BLK)]

    sides = ((0, a_next, to_y), (1, b_next, to_x))
    for n, piece, to in sides:
        for s, part in signs:
            link.send((n, "raw2", s), piece(2, part), c_raw.at[n, part], to(s))
    for n, piece, to in sides:
        for s, part in signs:
            link.send((n, "own2", s), piece(s, 1 - part), c_mid.at[n, part, 1 - part], to(s))
    for n, piece, to in sides:
        for s, part in signs:
            link.arrived((n, "raw2", s), c_raw.at[n, part], to(-s))
            c_out[n, part] = (c_raw[n, part].astype(F32) + piece(s, part)[...].astype(F32)).astype(BF16)
            link.send((n, "sum2", s), c_out.at[n, part], c_mid.at[n, part, part], to(s))
    for n, piece, to in sides:
        for s, part in signs:
            link.arrived((n, "own2", s), c_mid.at[n, part, 1 - part], to(-s))
            link.arrived((n, "sum2", s), c_mid.at[n, part, part], to(-s))
        total = piece(0, None)[...].astype(F32)
        total = total + c_mid[n, 0].reshape(half_rows, BLK).astype(F32) + c_mid[n, 1].reshape(half_rows, BLK).astype(F32)
        out[pl.ds(al(y * RB + n * half_rows, 64), half_rows), own] = total.astype(BF16)

    def region(half, x, y, part):
        first, count = ((0, half_rows), (0, quarter), (quarter, quarter))[0 if part is None else 1 + part]
        return out.at[
            pl.ds(al(y * RB + half * half_rows + first, quarter), count),
            pl.ds(al(x * BLK, 128), BLK),
        ]

    all_gather_2d(link, region)
    link.drain()


def merger_sum(tokens, up, up_bias, src, down, text):
    vmem = pl.BlockSpec(memory_space=pltpu.VMEM)
    half_rows = RB // 2
    return pl.pallas_call(
        merger_kernel,
        out_shape=jax.ShapeDtypeStruct((TOK_SEQ, WIDTH), BF16),
        in_specs=[vmem] * 6,
        out_specs=vmem,
        scratch_shapes=[
            pltpu.VMEM((ROWS, HID), F32),
            pltpu.VMEM((TOK_SEQ, HID), BF16),
            pltpu.VMEM((SIDE, RB, WIDTH), BF16),
            pltpu.VMEM((2, 2, half_rows, BLK), BF16),
            pltpu.VMEM((2, SIDE, half_rows, BLK), BF16),
            pltpu.VMEM((2, 2, half_rows, BLK), BF16),
            pltpu.VMEM((SIDE, half_rows, BLK), BF16),
            pltpu.VMEM((2, half_rows, WIDTH // 2), BF16),
            pltpu.VMEM((2, half_rows, WIDTH), BF16),
            pltpu.VMEM((2, half_rows, WIDTH // 2), BF16),
            pltpu.VMEM((half_rows, WIDTH), BF16),
            pltpu.VMEM((2, 2, half_rows // 2, BLK), BF16),
            pltpu.VMEM((2, 2, 2, half_rows // 2, BLK), BF16),
            pltpu.VMEM((2, 2, half_rows // 2, BLK), BF16),
            pltpu.SemaphoreType.DMA((AG_SEMS + 24,)),
            pltpu.SemaphoreType.DMA((AG_SEMS + 24,)),
        ],
        compiler_params=pltpu.CompilerParams(collective_id=1, has_side_effects=True),
        name="merger",
    )(tokens, up, up_bias, src, down, text)


def kv_kernel(own, out, send_sem, recv_sem):
    s = lax.axis_index("seq")
    z, core = s // 2, lax.rem(s, 2)

    def at(dz, dc):
        return lax.rem(z + dz + SIDE, SIDE) * 2 + lax.rem(core + dc, 2)

    greet([at(1, 0), at(-1, 0), at(0, 1)], "seq")
    link = Link(send_sem, recv_sem, "seq")
    part_rows = TOK_SEQ // 2

    def reg(dz, dc, part):
        b = at(dz, dc)
        return out.at[b] if part is None else out.at[b, pl.ds(part * part_rows, part_rows)]

    signs = ((1, 0), (-1, 1))
    for sg, _ in signs:
        link.send(("z", sg), own, reg(0, 0, None), at(sg, 0))
    link.send(("c", 0), own, reg(0, 0, None), at(0, 1))
    out[s] = own[...]
    for sg, part in signs:
        link.arrived(("z", sg), reg(-sg, 0, None), at(-sg, 0))
        link.send(("r", sg), reg(-sg, 0, part), reg(-sg, 0, part), at(sg, 0))
        link.send(("c", -sg), reg(-sg, 0, None), reg(-sg, 0, None), at(0, 1))
    for sg, part in signs:
        link.arrived(("r", sg), reg(2, 0, part), at(-sg, 0))
        link.send(("c", 2, part), reg(2, 0, part), reg(2, 0, part), at(0, 1))
    for dz in (0, -1, 1):
        link.arrived(("c", dz), reg(dz, 1, None), at(0, 1))
    for part in (0, 1):
        link.arrived(("c", 2, part), reg(2, 1, part), at(0, 1))
    link.drain()


def gather_kv(own):
    vmem = pl.BlockSpec(memory_space=pltpu.VMEM)
    return pl.pallas_call(
        kv_kernel,
        out_shape=jax.ShapeDtypeStruct((N_SEQ, TOK_SEQ, 2 * HEAD_DIMENSION), BF16),
        in_specs=[vmem],
        out_specs=vmem,
        scratch_shapes=[pltpu.SemaphoreType.DMA((9,)), pltpu.SemaphoreType.DMA((9,))],
        compiler_params=pltpu.CompilerParams(collective_id=2, has_side_effects=True),
        name="kv",
    )(own)


def heads_kernel(own, out, send_sem, recv_sem):
    t, x, y = place()
    greet(ring_peers())
    link = Link(send_sem, recv_sem)
    out[:, pl.ds(al(t * HEAD_DIMENSION, 128), HEAD_DIMENSION)] = own[...]

    def region(half, x, y, part):
        first, count = ((0, 256), (0, 128), (128, 128))[0 if part is None else 1 + part]
        return out.at[pl.ds(half * 256 + first, count), pl.ds(al((x * SIDE + y) * HEAD_DIMENSION, 128), HEAD_DIMENSION)]

    all_gather_2d(link, region)
    link.drain()


def gather_heads(own):
    vmem = pl.BlockSpec(memory_space=pltpu.VMEM)
    return pl.pallas_call(
        heads_kernel,
        out_shape=jax.ShapeDtypeStruct((TOK_SEQ, LOCAL_QUERY_HEAD * HEAD_DIMENSION), BF16),
        in_specs=[vmem],
        out_specs=vmem,
        scratch_shapes=[pltpu.SemaphoreType.DMA((AG_SEMS,)), pltpu.SemaphoreType.DMA((AG_SEMS,))],
        compiler_params=pltpu.CompilerParams(collective_id=3, has_side_effects=True),
        name="heads",
    )(own)


def image_fields(image_table):
    grid_h = image_table[:, 0]
    grid_w = image_table[:, 1]
    across = grid_w // 2
    return (across, grid_h // 2 * across, image_table[:, 2])


def rope_tables(positions, across, counts, offsets, head_size):
    inside = (
        (positions[:, None] >= offsets[None, :]) & (positions[:, None] < (offsets + counts)[None, :])
    ).astype(jnp.int32)
    is_image = jnp.sum(inside, axis=1)
    run_start = jnp.sum(inside * offsets[None, :], axis=1)
    row_width = jnp.sum(inside * across[None, :], axis=1) + (1 - is_image)
    inner_index = positions - run_start
    pos_t = jnp.where(is_image > 0, run_start, positions)
    pos_h = jnp.where(is_image > 0, run_start + inner_index // row_width, positions)
    pos_w = jnp.where(is_image > 0, run_start + inner_index % row_width, positions)
    half_size = head_size // 2
    frequency = jnp.arange(half_size, dtype=jnp.int32)
    inverse = THETA ** (-2.0 * frequency.astype(F32) / head_size)
    first_cut = head_size // 8
    second_cut = first_cut + 3 * head_size // 16
    chosen = jnp.where(
        frequency[None, :] < first_cut,
        pos_t[:, None],
        jnp.where(frequency[None, :] < second_cut, pos_h[:, None], pos_w[:, None]),
    )
    angles = chosen.astype(F32) * inverse[None, :]
    angles = jnp.concatenate([angles, angles], axis=1)
    return (jnp.cos(angles), jnp.sin(angles), is_image)


def rotate(value, cosine, sine):
    half = value.shape[-1] // 2
    turned = jnp.concatenate([-value[:, half:], value[:, :half]], axis=-1)
    return value * cosine + turned * sine


def per_device(
    patches, image_table, ln_gain, ln_bias, merge_up, merge_up_bias, merge_down, merge_down_bias,
    text_embeds, attn_gain, q_weight, q_bias, key_value_weight, key_value_bias, o_weight,
):
    seq_index = lax.axis_index("seq")
    t = lax.axis_index("tp")
    positions = seq_index * TOK_SEQ + jnp.arange(TOK_SEQ, dtype=jnp.int32)
    begin = 2 * seq_index * N_TP
    group = lax.dynamic_slice_in_dim(image_table, begin, 2 * N_TP)
    across, counts, offsets = image_fields(group)
    cosine, sine, is_image = rope_tables(positions, across, counts, offsets, HEAD_DIMENSION)
    mask = is_image.astype(F32)
    starts = offsets.reshape(N_TP, 2)[:, 0]
    lengths = jnp.sum(counts.reshape(N_TP, 2), axis=1)
    devices = jnp.arange(N_TP, dtype=jnp.int32)
    base = jnp.sum(jnp.where(devices[None, :] < devices[:, None], lengths[None, :], 0), axis=1)
    k = jnp.arange(32, dtype=jnp.int32)
    mine = (devices == t).astype(jnp.int32)
    my_base, my_length = jnp.sum(mine * base), jnp.sum(mine * lengths)
    parity = jnp.arange(2, dtype=jnp.int32)
    token = 2 * k[None, :] + ((parity + my_base) % 2)[:, None]
    src_row = jnp.where(token < my_length, 4 * token, -8).reshape(CAP, 1)
    taken = 2 * k[None, :] + ((t + base) % 2)[:, None]
    target = jnp.where(taken < lengths[:, None], (base[:, None] + taken) // 2, -1).reshape(1, N_TP * 32)
    inner = positions[:, None] - starts[None, :]
    within = (inner >= 0) & (inner < lengths[None, :])
    compact = jnp.sum(jnp.where(within, base[None, :] + inner, 0), axis=1)
    src = jnp.where(is_image > 0, compact % 2 * 2 * HALF + compact // 2, -1).reshape(TOK_SEQ, 1)

    tokens = gather_tokens(patches, ln_gain.reshape(1, VW), ln_bias.reshape(1, VW), src_row, target)
    text = jnp.where(is_image[:, None] > 0, 0, text_embeds).astype(BF16)
    weight_cols = lax.all_to_all(
        o_weight, "tp", split_axis=1, concat_axis=0, tiled=True
    )
    summed = merger_sum(tokens, merge_up, merge_up_bias.reshape(1, HID), src, merge_down, text)
    residual = summed.astype(F32) + mask[:, None] * merge_down_bias[None, :]
    scale_rows = lax.rsqrt(jnp.mean(residual * residual, axis=1) + EPS)
    normed_rows = (residual * scale_rows[:, None] * attn_gain[None, :]).astype(BF16)

    kv_head = t * KEY_VALUE_HEADS // LOCAL_QUERY_HEAD
    key_at = kv_head * HEAD_DIMENSION
    value_at = KEY_VALUE_HEADS * HEAD_DIMENSION + key_at
    key_weight = lax.dynamic_slice_in_dim(key_value_weight, key_at, HEAD_DIMENSION, 1)
    value_weight = lax.dynamic_slice_in_dim(key_value_weight, value_at, HEAD_DIMENSION, 1)
    key_bias = lax.dynamic_slice_in_dim(key_value_bias, key_at, HEAD_DIMENSION)
    value_bias = lax.dynamic_slice_in_dim(key_value_bias, value_at, HEAD_DIMENSION)
    key = jnp.dot(normed_rows, key_weight, preferred_element_type=F32) + key_bias
    value = jnp.dot(normed_rows, value_weight, preferred_element_type=F32) + value_bias
    query = jnp.dot(normed_rows, q_weight, preferred_element_type=F32) + q_bias
    key = rotate(key, cosine, sine).astype(BF16)
    query = rotate(query, cosine, sine).astype(BF16)
    pieces = gather_kv(jnp.concatenate([key, value.astype(BF16)], axis=1))
    pieces = pieces.reshape(N_SEQ * TOK_SEQ, 2 * HEAD_DIMENSION)
    keys, values = pieces[:, :HEAD_DIMENSION], pieces[:, HEAD_DIMENSION:]
    key_position = jnp.arange(N_SEQ * TOK_SEQ, dtype=jnp.int32)
    scores = jnp.einsum("qd,kd->qk", query, keys, preferred_element_type=F32) * HEAD_DIMENSION ** (-0.5)
    allowed = key_position[None, :] <= positions[:, None]
    scores = jnp.where(allowed, scores, -1e30)
    best = jnp.max(scores, axis=1)
    weights = jnp.where(allowed, jnp.exp(scores - best[:, None]), 0.0)
    total = jnp.sum(weights, axis=1)
    acc = jnp.dot(weights.astype(BF16), values, preferred_element_type=F32)
    attention = (acc / total[:, None]).astype(BF16)
    gathered = gather_heads(attention)
    mixed = jnp.dot(gathered, weight_cols, preferred_element_type=F32)
    own_columns = lax.dynamic_slice_in_dim(summed, t * COLS, COLS, 1).astype(F32)
    own_bias = lax.dynamic_slice_in_dim(merge_down_bias, t * COLS, COLS)
    return (own_columns + mask[:, None] * own_bias[None, :] + mixed).astype(BF16)


def solution(mesh):
    return jax.shard_map(
        per_device,
        mesh=mesh,
        in_specs=(
            P(("seq", "tp"), None),
            P(),
            P(),
            P(),
            P(None, "tp"),
            P("tp"),
            P("tp", None),
            P(),
            P("seq", "tp"),
            P(),
            P(None, "tp"),
            P("tp"),
            P(),
            P(),
            P("tp", None),
        ),
        out_specs=P("seq", "tp"),
        check_vma=False,
    )
```

```python
import functools

import jax
import jax.numpy as jnp
from jax import lax
from jax.experimental import pallas as pl
from jax.experimental.pallas import tpu as pltpu
from jax.sharding import PartitionSpec as P

MESH = pl.DeviceIdType.MESH
HEAD_DIMENSION = 128
KEY_VALUE_HEADS = 4
LOCAL_QUERY_HEAD = 16
CAP = 64
TOK_SEQ = 512
MW = 5120
VW = 1280
WIDTH = 3584
HID = 320
COLS = 224
N_TP = 16
N_SEQ = 8
SIDE = 4
ROWS = 448
HALF = 112
TCOL = 640
BLK = 896
RB = 128

EPS = 1e-06
THETA = 1000000.0
F32 = jnp.float32
BF16 = jnp.bfloat16


def al(value, multiple):
    return pl.multiple_of(value, multiple)


def place():
    t = lax.axis_index("tp")
    return t, t // SIDE, lax.rem(t, SIDE)


def wrap(value):
    return lax.rem(value + 2 * SIDE, SIDE)


def at_xy(x, y):
    return wrap(x) * SIDE + wrap(y)


def offset_xy(half, i, j):
    t, x, y = place()
    return (wrap(x + j), wrap(y + i)) if half == 0 else (wrap(x + i), wrap(y + j))


def peer(half, phase, sign):
    x, y = offset_xy(half, sign, 0) if phase == 1 else offset_xy(half, 0, sign)
    return x * SIDE + y


class Link:
    def __init__(self, send_sem, recv_sem, axis="tp"):
        self.send_sem, self.recv_sem, self.axis = send_sem, recv_sem, axis
        self.number, self.open = {}, []

    def _copy(self, key, src, dst, device):
        k = self.number.setdefault(key, len(self.number))
        return pltpu.make_async_remote_copy(
            src_ref=src,
            dst_ref=dst,
            send_sem=self.send_sem.at[k],
            recv_sem=self.recv_sem.at[k],
            device_id={self.axis: device},
            device_id_type=MESH,
        )

    def send(self, key, src, dst, device):
        copy = self._copy(key, src, dst, device)
        copy.start()
        self.open.append(copy)

    def arrived(self, key, dst, device):
        self._copy(key, dst, dst, device).wait_recv()

    def drain(self):
        assert len(self.number) <= self.send_sem.shape[0]
        for copy in self.open:
            copy.wait_send()
        self.open = []


def all_gather_2d(link, region, tag, own=None, hooks=(), lead=0):
    def reg(half, i, j, part):
        x, y = offset_xy(half, i, j)
        return region(half, x, y, part)

    def send(key, half, phase, sign, i, j, part):
        ref = reg(half, i, j, part)
        src = own(half) if own is not None and i == 0 and j == 0 else ref
        link.send((tag, half, *key), src, ref, peer(half, phase, sign))

    def got(key, half, phase, sign, i, j, part):
        link.arrived((tag, half, *key), reg(half, i, j, part), peer(half, phase, -sign))

    both = ((1, 0), (-1, 1))
    halves = (0, 1)

    def last(i, h):
        for s, part in both:
            got(("r2", s, i), h, 2, s, i, 2, part)

    for h in halves:
        for s, _ in both:
            send(("p1", s), h, 1, s, 0, 0, None)
    for h in halves:
        for s, _ in both:
            send(("p2", s, 0), h, 2, s, 0, 0, None)
    for s, part in both:
        for h in halves:
            got(("p1", s), h, 1, s, -s, 0, None)
            send(("r1", s), h, 1, s, -s, 0, part)
            for s2, _ in both:
                send(("p2", s2, -s), h, 2, s2, -s, 0, None)
    for s, part in both:
        for h in halves:
            got(("p2", s, 0), h, 2, s, 0, -s, None)
            send(("r2", s, 0), h, 2, s, 0, -s, part)
    for s, part in both:
        for h in halves:
            got(("r1", s), h, 1, s, 2, 0, part)
            for s2, _ in both:
                send(("p2", s2, 2, part), h, 2, s2, 2, 0, part)
    for i in (-1, 1):
        for s, part in both:
            for h in halves:
                got(("p2", s, i), h, 2, s, i, -s, None)
                send(("r2", s, i), h, 2, s, i, -s, part)
    last(0, lead)
    if hooks:
        hooks[0]()
    for s, part in both:
        for h in halves:
            got(("p2", s, 2, part), h, 2, s, 2, -s, part)
            send(("r2", s, 2), h, 2, s, 2, -s, part)
    for s, part in both:
        for h in halves:
            got(("p2", s, 2, 1 - part), h, 2, s, 2, -s, 1 - part)
    for n, i in enumerate((-1, 1)):
        last(i, lead)
        if hooks:
            hooks[1 + n]()
    last(2, lead)
    for i in (0, -1, 1, 2):
        last(i, 1 - lead)
    if hooks:
        hooks[3]()


AG_SEMS = 44


ORDER = (0, -1, 1, 2)
SIGNS = ((1, 0), (-1, 1))
HROW = RB // 2
QROW = RB // 4
D = HEAD_DIMENSION


def chosen(index, pieces):
    value = pieces[0]
    for k in range(1, len(pieces)):
        value = jnp.where(index == k, pieces[k], value)
    return value


def row_of(ref):
    return ref[...].reshape(1, ref.shape[0])


def layout(table, s):
    start, length, base = [], [], []
    so_far = 0
    for e in range(N_TP):
        i = 2 * N_TP * s + 2 * e
        first = (table[0, i] // 2) * (table[1, i] // 2)
        second = (table[0, i + 1] // 2) * (table[1, i + 1] // 2)
        start.append(table[2, i])
        length.append(first + second)
        base.append(so_far)
        so_far = so_far + first + second
    return start, length, base


def body(
    table, patches, ln_gain, ln_bias, up_hbm, up_bias, down_hbm, down_bias, text, gain, q_weight, q_bias,
    kv_weight, kv_bias, o_hbm, cosine, sine, out,
    up, down, o_rows, o_send, o_cols, outgoing, incoming, tokens, lifted, hidden, pa, pb,
    a_raw, a_mid, a_out, a_sum, b_raw, b_mid, b_out, b_sum, c_raw, c_mid, c_out, shard,
    rows_ref, weight, normed, query, kv, heads, best, total, acc, load_sem, send_sem, recv_sem, seq_send, seq_recv,
):
    t, x, y = place()
    s = lax.axis_index("seq")
    z, core = s // 2, lax.rem(s, 2)

    def at(dz, dc):
        return lax.rem(z + dz + SIDE, SIDE) * 2 + lax.rem(core + dc, 2)

    barrier = pltpu.get_barrier_semaphore()
    for o in range(1, N_TP):
        pl.semaphore_signal(barrier, inc=1, device_id={"tp": lax.rem(t + o, N_TP)}, device_id_type=MESH)
    for device in (at(1, 0), at(-1, 0), at(0, 1)):
        pl.semaphore_signal(barrier, inc=1, device_id={"seq": device}, device_id_type=MESH)

    def load(n, src, dst):
        copy = pltpu.make_async_copy(src, dst, load_sem.at[n])
        copy.start()
        return copy

    load_o = load(0, o_hbm.at[pl.ds(al(s * 16, 16), 16), :], o_rows)
    load_up = load(1, up_hbm, up)
    load_down = load(2, down_hbm, down)
    load_qkv = [
        load(3, q_weight, weight.at[:, pl.ds(0, D)]),
        load(4, kv_weight.at[:, pl.ds(al(x * D, 128), D)], weight.at[:, pl.ds(D, D)]),
        load(5, kv_weight.at[:, pl.ds(al((KEY_VALUE_HEADS + x) * D, 128), D)], weight.at[:, pl.ds(2 * D, D)]),
    ]
    link = Link(send_sem, recv_sem)
    along = Link(seq_send, seq_recv, "seq")
    start, length, base = layout(table, s)

    value = patches[...].astype(F32)
    centre = jnp.mean(value, axis=-1, keepdims=True)
    centred = value - centre
    spread = jnp.mean(centred * centred, axis=-1, keepdims=True)
    fine = (centred * lax.rsqrt(spread + EPS) * row_of(ln_gain) + row_of(ln_bias)).astype(BF16)
    my_base, my_length = chosen(t, base), chosen(t, length)
    slot = lax.broadcasted_iota(jnp.int32, (CAP, 4 * CAP), 0)
    lane = lax.broadcasted_iota(jnp.int32, (CAP, 4 * CAP), 1)
    token = 2 * lax.rem(slot, 32) + lax.rem(slot // 32 + my_base, 2)
    source = jnp.where(token < my_length, 4 * token, -8)
    pl.semaphore_wait(barrier, N_TP + 2)
    for i in (1, 2, 3, 0):
        q = wrap(x + i)
        part = jnp.dot((lane == source + q).astype(BF16), fine, preferred_element_type=F32).astype(BF16)
        for u in range(2):
            for r in range(2):
                outgoing[4 * q + 2 * u + r] = part[r * 32 : (r + 1) * 32, u * TCOL : (u + 1) * TCOL]
        for j in (1, 2, 3, 0):
            if (i, j) != (0, 0):
                to = at_xy(x + i, y + j)
                link.send(("a", i, j), outgoing.at[to], incoming.at[t], to)
    incoming[t] = outgoing[t]

    load_o.wait()
    o_all = o_rows[...]
    for d in range(N_TP):
        o_send[d] = o_all[:, d * COLS : (d + 1) * COLS]
    o_place = pl.ds(al(s * 16, 16), 16)
    for o in range(1, N_TP):
        to = lax.rem(t + o, N_TP)
        link.send(("o", o), o_send.at[to], o_cols.at[t, o_place, :], to)
    o_cols[t, o_place, :] = o_send[t]

    half_of = lax.rem(t, 2)
    lane = lax.broadcasted_iota(jnp.int32, (1, N_TP * 32), 1)
    base_row = jnp.zeros((1, N_TP * 32), jnp.int32)
    length_row = base_row
    for e in range(N_TP):
        here = lane // 32 == e
        base_row = jnp.where(here, base[e], base_row)
        length_row = jnp.where(here, length[e], length_row)
    taken = 2 * lax.rem(lane, 32) + lax.rem(half_of + base_row, 2)
    target = jnp.where(taken < length_row, (base_row + taken) // 2, -1)
    pick = (lax.broadcasted_iota(jnp.int32, (2 * HALF, N_TP * 32), 0) == target).astype(BF16)
    for i in (1, 2, 3, 0):
        for j in (1, 2, 3, 0):
            if (i, j) != (0, 0):
                frm = at_xy(x - i, y - j)
                link.arrived(("a", i, j), incoming.at[frm], frm)
    slots = incoming[...].reshape(N_TP * 32, TCOL)
    mine = jnp.dot(pick, slots, preferred_element_type=F32).astype(BF16)
    tokens[pl.ds(al(half_of * 2 * HALF, 2 * HALF), 2 * HALF), pl.ds(al(t // 2 * TCOL, 128), TCOL)] = mine

    def token_region(half, x, y, part):
        d = x * SIDE + y
        first, width = ((0, TCOL), (0, 384), (384, 256))[0 if part is None else 1 + part]
        return tokens.at[
            pl.ds(al(lax.rem(d, 2) * 2 * HALF + half * HALF, 16), HALF),
            pl.ds(al(d // 2 * TCOL + first, 128), width),
        ]

    def o_region(dz, dc, part):
        first, count = ((0, N_TP), (0, 8), (8, 8))[0 if part is None else 1 + part]
        return o_cols.at[pl.ds(first, count), pl.ds(al(at(dz, dc) * 16, 16), 16), :]

    def lift(n):
        cols = pl.ds(al(wrap(x + ORDER[n]) * VW, 128), VW)
        got = lax.dot_general(
            tokens[:, cols], up[:, cols], (((1,), (1,)), ((), ())), preferred_element_type=F32
        )
        if n == 0:
            lifted[...] = got + row_of(up_bias)
        else:
            lifted[...] += got

    def lift_first():
        load_up.wait()
        lift(0)
        for o in range(1, N_TP):
            frm = lax.rem(t - o + N_TP, N_TP)
            link.arrived(("o", o), o_cols.at[frm, o_place, :], frm)
        for sg, _ in SIGNS:
            along.send(("o", "z", sg), o_region(0, 0, None), o_region(0, 0, None), at(sg, 0))
        along.send(("o", "c", 0), o_region(0, 0, None), o_region(0, 0, None), at(0, 1))

    all_gather_2d(
        link, token_region, "t", None,
        (lift_first, functools.partial(lift, 1), functools.partial(lift, 2), functools.partial(lift, 3)), 1,
    )

    raised = lifted[...]
    act = (0.5 * raised * (1.0 + lax.erf(raised * 0.5**0.5))).astype(BF16)
    order = lax.broadcasted_iota(jnp.int32, (TOK_SEQ, 1), 0)
    pos = s * TOK_SEQ + lax.rem(order, 256) // HROW * RB + order // 256 * HROW + lax.rem(order, HROW)
    where = jnp.full((TOK_SEQ, 1), -1, jnp.int32)
    for e in range(N_TP):
        inner = pos - start[e]
        where = jnp.where((inner >= 0) & (inner < length[e]), base[e] + inner, where)
    where = jnp.where(where >= 0, lax.rem(where, 2) * 2 * HALF + where // 2, -1)
    pick = (lax.broadcasted_iota(jnp.int32, (TOK_SEQ, ROWS), 1) == where).astype(BF16)
    hidden[...] = jnp.dot(pick, act, preferred_element_type=F32).astype(BF16)
    load_down.wait()
    spot = (
        lax.broadcasted_iota(jnp.int32, (COLS, BLK), 0) + y * COLS == lax.broadcasted_iota(jnp.int32, (COLS, BLK), 1)
    ).astype(BF16)
    own = pl.ds(al(x * BLK, 128), BLK)
    at_lane = s * TOK_SEQ + lax.broadcasted_iota(jnp.int32, (1, TOK_SEQ), 1)
    plain = jnp.ones((1, TOK_SEQ), F32)
    for e in range(N_TP):
        plain = jnp.where((at_lane >= start[e]) & (at_lane < start[e] + length[e]), 0.0, plain)
    words = (text[...].astype(F32) * plain).astype(BF16)

    def words_of(rb):
        return lax.dot_general(
            words[:, rb * RB : (rb + 1) * RB], spot, (((0,), (0,)), ((), ())), preferred_element_type=F32
        )

    def lower_a(i):
        cols = pl.ds(al(wrap(x + i) * BLK, 128), BLK)
        got = jnp.dot(hidden[0:256, :], down[:, cols], preferred_element_type=F32)
        pa[:, :, cols] = got.astype(BF16).reshape(SIDE, HROW, BLK)

    def lower_b(i):
        rb = wrap(y + i)
        got = jnp.dot(hidden[pl.ds(al(256 + rb * HROW, HROW), HROW), :], down[...], preferred_element_type=F32)
        pb[rb] = got.astype(BF16)

    for rb in range(SIDE):
        add = words_of(rb)
        a_add = add[:HROW]
        pb_add = add[HROW:]
        a_sum[rb] = a_add.astype(BF16)
        b_words = pb_add.astype(BF16)
        b_sum[pl.ds(0, HROW), pl.ds(rb * BLK, BLK)] = b_words

    def a_piece(i, part):
        rows = (pl.ds(0, SIDE), pl.ds(0, 2), pl.ds(2, 2))[0 if part is None else 1 + part]
        return pa.at[rows, :, pl.ds(al(wrap(x + i) * BLK, 128), BLK)]

    def b_piece(i, part):
        cols = (pl.ds(0, WIDTH), pl.ds(0, WIDTH // 2), pl.ds(WIDTH // 2, WIDTH // 2))[0 if part is None else 1 + part]
        return pb.at[wrap(y + i), :, cols]

    def to_x(sg):
        return at_xy(x + sg, y)

    def to_y(sg):
        return at_xy(x, y + sg)

    def mid_of(ref, name, part):
        if name == "a":
            return ref.at[pl.ds(2 * part, 2)]
        return ref.at[:, pl.ds(part * (WIDTH // 2), WIDTH // 2)]

    def make_a(i):
        lower_a(i)
        if i == 0:
            pa[:, :, own] = (pa[:, :, own].astype(F32) + a_sum[...].astype(F32)).astype(BF16)

    def make_b(i):
        lower_b(i)
        rb = wrap(y + i)
        add = b_sum[:, pl.ds(al(rb * BLK, 128), BLK)].astype(F32)
        pb[rb, :, own] = (pb[rb, :, own].astype(F32) + add).astype(BF16)

    sides = (
        ("a", a_piece, a_raw, a_mid, a_out, to_x, make_a),
        ("b", b_piece, b_raw, b_mid, b_out, to_y, make_b),
    )
    for n, piece, raw, mid, outb, to, make in sides:
        make(2)
        for sg, part in SIGNS:
            link.send((n, "raw", sg), piece(2, part), raw.at[part], to(sg))
    for sg, part in SIGNS:
        for n, piece, raw, mid, outb, to, make in sides:
            make(sg)
            link.send((n, "own", sg), piece(sg, 1 - part), mid_of(mid.at[part], n, 1 - part), to(sg))
    for n, piece, raw, mid, outb, to, make in sides:
        for sg, part in SIGNS:
            link.arrived((n, "raw", sg), raw.at[part], to(-sg))
            outb[part] = (raw[part].astype(F32) + piece(sg, part)[...].astype(F32)).astype(BF16)
            link.send((n, "sum", sg), outb.at[part], mid_of(mid.at[part], n, part), to(sg))
    for n, piece, raw, mid, outb, to, make in sides:
        make(0)

    for sg, part in SIGNS:
        along.arrived(("o", "z", sg), o_region(-sg, 0, None), at(-sg, 0))
        along.send(("o", "r", sg), o_region(-sg, 0, part), o_region(-sg, 0, part), at(sg, 0))
        along.send(("o", "c", -sg), o_region(-sg, 0, None), o_region(-sg, 0, None), at(0, 1))

    def a_next(i, part):
        rows = (pl.ds(0, HROW), pl.ds(0, QROW), pl.ds(QROW, QROW))[0 if part is None else 1 + part]
        return a_sum.at[wrap(y + i), rows, :]

    def b_next(i, part):
        rows = (pl.ds(0, HROW), pl.ds(0, QROW), pl.ds(QROW, QROW))[0 if part is None else 1 + part]
        return b_sum.at[rows, pl.ds(al(wrap(x + i) * BLK, 128), BLK)]

    after = ((0, a_next, to_y), (1, b_next, to_x))
    for side, nxt in zip(sides, after):
        n, piece, raw, mid, outb, to, make = side
        for sg, part in SIGNS:
            link.arrived((n, "own", sg), mid_of(mid.at[part], n, 1 - part), to(-sg))
            link.arrived((n, "sum", sg), mid_of(mid.at[part], n, part), to(-sg))
        held = a_sum if n == "a" else b_sum
        held[...] = (piece(0, None)[...].astype(F32) + mid[0].astype(F32) + mid[1].astype(F32)).astype(BF16)
        n, piece, to = nxt
        for sg, part in SIGNS:
            link.send((n, "raw2", sg), piece(2, part), c_raw.at[n, part], to(sg))
        for sg, part in SIGNS:
            link.send((n, "own2", sg), piece(sg, 1 - part), c_mid.at[n, part, 1 - part], to(sg))
    for n, piece, to in after:
        for sg, part in SIGNS:
            link.arrived((n, "raw2", sg), c_raw.at[n, part], to(-sg))
            c_out[n, part] = (c_raw[n, part].astype(F32) + piece(sg, part)[...].astype(F32)).astype(BF16)
            link.send((n, "sum2", sg), c_out.at[n, part], c_mid.at[n, part, part], to(sg))
    row = s * TOK_SEQ + y * RB + lax.broadcasted_iota(jnp.int32, (RB, 1), 0)
    image = jnp.zeros((RB, 1), F32)
    for e in range(N_TP):
        image = jnp.where((row >= start[e]) & (row < start[e] + length[e]), 1.0, image)
    full_bias = row_of(down_bias)
    shift = image * chosen(x, [full_bias[:, k * BLK : (k + 1) * BLK] for k in range(SIDE)])
    for n, piece, to in after:
        for sg, part in SIGNS:
            link.arrived((n, "own2", sg), c_mid.at[n, part, 1 - part], to(-sg))
            link.arrived((n, "sum2", sg), c_mid.at[n, part, part], to(-sg))
        held = piece(0, None)[...].astype(F32)
        held = held + c_mid[n, 0].reshape(HROW, BLK).astype(F32) + c_mid[n, 1].reshape(HROW, BLK).astype(F32)
        shard[pl.ds(n * HROW, HROW), :] = (held + shift[n * HROW : (n + 1) * HROW]).astype(BF16)

    for sg, part in SIGNS:
        along.arrived(("o", "r", sg), o_region(2, 0, part), at(-sg, 0))
        along.send(("o", "c", 2, part), o_region(2, 0, part), o_region(2, 0, part), at(0, 1))

    def region(half, x, y, part):
        first, count = ((0, HROW), (0, QROW), (QROW, QROW))[0 if part is None else 1 + part]
        return rows_ref.at[
            pl.ds(al(y * RB + half * HROW + first, QROW), count),
            pl.ds(al(x * BLK, 128), BLK),
        ]

    def kv_at(n, dz, dc, part):
        first, count = ((0, RB), (0, HROW), (HROW, HROW))[0 if part is None else 1 + part]
        return kv.at[at(dz, dc), pl.ds(al(wrap(y + ORDER[n]) * RB + first, HROW), count), :]

    kv_row = row_of(kv_bias)
    heads_of = [kv_row[:, k * D : (k + 1) * D] for k in range(2 * KEY_VALUE_HEADS)]
    key_bias, value_bias = chosen(x, heads_of[:KEY_VALUE_HEADS]), chosen(x, heads_of[KEY_VALUE_HEADS:])

    def project(n):
        rows = pl.ds(al(wrap(y + ORDER[n]) * RB, RB), RB)
        value = rows_ref[rows, :].astype(F32)
        scale = lax.rsqrt(jnp.mean(value * value, axis=-1, keepdims=True) + EPS)
        normed[...] = (value * scale * row_of(gain)).astype(BF16)
        got = jnp.dot(normed[...], weight[...], preferred_element_type=F32)
        c, sn = cosine[rows, :], sine[rows, :]
        q, k = got[:, :D] + row_of(q_bias), got[:, D : 2 * D] + key_bias
        kv[s, rows, 0:D] = (k * c + pltpu.roll(k, D // 2, 1) * sn).astype(BF16)
        kv[s, rows, D : 2 * D] = (got[:, 2 * D :] + value_bias).astype(BF16)
        for sg, _ in SIGNS:
            along.send((n, "z", sg), kv_at(n, 0, 0, None), kv_at(n, 0, 0, None), at(sg, 0))
        along.send((n, "c", 0), kv_at(n, 0, 0, None), kv_at(n, 0, 0, None), at(0, 1))
        query[rows, :] = (q * c + pltpu.roll(q, D // 2, 1) * sn).astype(BF16)

    def relay(n):
        for sg, part in SIGNS:
            along.arrived((n, "z", sg), kv_at(n, -sg, 0, None), at(-sg, 0))
            along.send((n, "r", sg), kv_at(n, -sg, 0, part), kv_at(n, -sg, 0, part), at(sg, 0))
            along.send((n, "c", -sg), kv_at(n, -sg, 0, None), kv_at(n, -sg, 0, None), at(0, 1))

    def first():
        for copy in load_qkv:
            copy.wait()
        project(0)

    def third():
        project(2)
        relay(0)

    def fourth():
        relay(1)
        project(3)
        relay(2)

    rows_ref[pl.ds(al(y * RB, RB), RB), own] = shard[...]
    all_gather_2d(
        link, region, "x", lambda half: shard.at[pl.ds(half * HROW, HROW)],
        (first, functools.partial(project, 1), third, fourth),
    )

    step = HEAD_DIMENSION ** (-0.5)
    chunk = 256

    def attend(b, causal):
        keys, values = kv[b, :, 0:D], kv[b, :, D : 2 * D]
        for r in range(TOK_SEQ // chunk):
            rows = slice(r * chunk, (r + 1) * chunk)
            width = (r + 1) * chunk if causal else TOK_SEQ
            score = lax.dot_general(query[rows, :], keys[:width], (((1,), (1,)), ((), ())), preferred_element_type=F32)
            if causal:
                down_row = lax.broadcasted_iota(jnp.int32, score.shape, 0) + r * chunk
                col = lax.broadcasted_iota(jnp.int32, score.shape, 1)
                score = jnp.where(col <= down_row, score, -1e30)
                top = jnp.max(score, axis=1, keepdims=True)
                p = jnp.exp((score - top) * step)
                total[rows, :] = jnp.sum(p, axis=1, keepdims=True)
                acc[rows, :] = jnp.dot(p.astype(BF16), values[:width], preferred_element_type=F32)
            else:
                old = best[rows, :]
                top = jnp.maximum(old, jnp.max(score, axis=1, keepdims=True))
                fade = jnp.exp((old - top) * step)
                p = jnp.exp((score - top) * step)
                total[rows, :] = total[rows, :] * fade + jnp.sum(p, axis=1, keepdims=True)
                acc[rows, :] = acc[rows, :] * fade + jnp.dot(p.astype(BF16), values, preferred_element_type=F32)
            best[rows, :] = top

    def attend_if(dz, dc):
        b = at(dz, dc)

        @pl.when(b < s)
        def _():
            attend(b, False)

    attend(s, True)
    relay(3)
    for n in range(4):
        along.arrived((n, "c", 0), kv_at(n, 0, 1, None), at(0, 1))
    attend_if(0, 1)
    for n in range(4):
        for sg, part in SIGNS:
            along.arrived((n, "r", sg), kv_at(n, 2, 0, part), at(-sg, 0))
            along.send((n, "c", 2, part), kv_at(n, 2, 0, part), kv_at(n, 2, 0, part), at(0, 1))
    for dz in (-1, 1):
        attend_if(dz, 0)
        for n in range(4):
            along.arrived((n, "c", dz), kv_at(n, dz, 1, None), at(0, 1))
        attend_if(dz, 1)
    attend_if(2, 0)
    for n in range(4):
        for part in (0, 1):
            along.arrived((n, "c", 2, part), kv_at(n, 2, 1, part), at(0, 1))
    attend_if(2, 1)
    heads[:, pl.ds(al(t * D, 128), D)] = (acc[...] / total[...]).astype(BF16)

    def head_region(half, x, y, part):
        first, count = ((0, 256), (0, 128), (128, 128))[0 if part is None else 1 + part]
        return heads.at[pl.ds(half * 256 + first, count), pl.ds(al((x * SIDE + y) * D, 128), D)]

    all_gather_2d(link, head_region, "h")
    for dz in (0, -1, 1):
        along.arrived(("o", "c", dz), o_region(dz, 1, None), at(0, 1))
    for part in (0, 1):
        along.arrived(("o", "c", 2, part), o_region(2, 1, part), at(0, 1))
    mine = lax.dot_general(rows_ref[:, own], spot, (((1,), (1,)), ((), ())), preferred_element_type=F32)
    last = o_cols[...].reshape(LOCAL_QUERY_HEAD * D, COLS)
    out[...] = (mine + jnp.dot(heads[...], last, preferred_element_type=F32)).astype(BF16)
    link.drain()
    along.drain()


LINKS = 3 * AG_SEMS + 30 + 24
ALONG = 45


def run(*operands):
    vmem = pl.BlockSpec(memory_space=pltpu.VMEM)
    hbm = pl.BlockSpec(memory_space=pl.ANY)
    smem = pl.BlockSpec(memory_space=pltpu.SMEM)

    def b16(*shape):
        return pltpu.VMEM(shape, BF16)

    def f32(*shape):
        return pltpu.VMEM(shape, F32)

    return pl.pallas_call(
        body,
        out_shape=jax.ShapeDtypeStruct((TOK_SEQ, COLS), BF16),
        in_specs=[
            smem, vmem, vmem, vmem, hbm, vmem, hbm, vmem, vmem, vmem, hbm, vmem, hbm, vmem, hbm, vmem, vmem
        ],
        out_specs=vmem,
        scratch_shapes=[
            b16(HID, MW), b16(HID, WIDTH), b16(16, WIDTH), b16(N_TP, 16, COLS), b16(N_TP, D, COLS),
            b16(N_TP, 32, TCOL), b16(N_TP, 32, TCOL), b16(ROWS, MW), f32(ROWS, HID), b16(TOK_SEQ, HID),
            b16(SIDE, HROW, WIDTH), b16(SIDE, HROW, WIDTH),
            b16(2, 2, HROW, BLK), b16(2, SIDE, HROW, BLK), b16(2, 2, HROW, BLK), b16(SIDE, HROW, BLK),
            b16(2, HROW, WIDTH // 2), b16(2, HROW, WIDTH), b16(2, HROW, WIDTH // 2), b16(HROW, WIDTH),
            b16(2, 2, QROW, BLK), b16(2, 2, 2, QROW, BLK), b16(2, 2, QROW, BLK), b16(RB, BLK),
            b16(TOK_SEQ, WIDTH), b16(WIDTH, 3 * D), b16(RB, WIDTH), b16(TOK_SEQ, D), b16(N_SEQ, TOK_SEQ, 2 * D),
            b16(TOK_SEQ, LOCAL_QUERY_HEAD * D), f32(TOK_SEQ, 1), f32(TOK_SEQ, 1), f32(TOK_SEQ, D),
            pltpu.SemaphoreType.DMA((6,)),
            pltpu.SemaphoreType.DMA((LINKS,)), pltpu.SemaphoreType.DMA((LINKS,)),
            pltpu.SemaphoreType.DMA((ALONG,)), pltpu.SemaphoreType.DMA((ALONG,)),
        ],
        compiler_params=pltpu.CompilerParams(
            collective_id=0, has_side_effects=True, vmem_limit_bytes=60 * 1024 * 1024
        ),
        name="block",
    )(*operands)


def image_fields(image_table):
    grid_h = image_table[:, 0]
    grid_w = image_table[:, 1]
    across = grid_w // 2
    return (across, grid_h // 2 * across, image_table[:, 2])


def rope_tables(positions, across, counts, offsets, head_size):
    inside = (
        (positions[:, None] >= offsets[None, :]) & (positions[:, None] < (offsets + counts)[None, :])
    ).astype(jnp.int32)
    is_image = jnp.sum(inside, axis=1)
    run_start = jnp.sum(inside * offsets[None, :], axis=1)
    row_width = jnp.sum(inside * across[None, :], axis=1) + (1 - is_image)
    inner_index = positions - run_start
    pos_t = jnp.where(is_image > 0, run_start, positions)
    pos_h = jnp.where(is_image > 0, run_start + inner_index // row_width, positions)
    pos_w = jnp.where(is_image > 0, run_start + inner_index % row_width, positions)
    half_size = head_size // 2
    frequency = jnp.arange(half_size, dtype=jnp.int32)
    inverse = THETA ** (-2.0 * frequency.astype(F32) / head_size)
    first_cut = head_size // 8
    second_cut = first_cut + 3 * head_size // 16
    chosen = jnp.where(
        frequency[None, :] < first_cut,
        pos_t[:, None],
        jnp.where(frequency[None, :] < second_cut, pos_h[:, None], pos_w[:, None]),
    )
    angles = chosen.astype(F32) * inverse[None, :]
    cosine, sine = jnp.cos(angles), jnp.sin(angles)
    return (jnp.concatenate([cosine, cosine], axis=1), jnp.concatenate([-sine, sine], axis=1))


def per_device(
    patches, image_table, ln_gain, ln_bias, merge_up, merge_up_bias, merge_down, merge_down_bias,
    text_embeds, attn_gain, q_weight, q_bias, key_value_weight, key_value_bias, o_weight,
):
    seq_index = lax.axis_index("seq")
    positions = seq_index * TOK_SEQ + jnp.arange(TOK_SEQ, dtype=jnp.int32)
    begin = 2 * seq_index * N_TP
    group = lax.dynamic_slice_in_dim(image_table, begin, 2 * N_TP)
    across, counts, offsets = image_fields(group)
    cosine, sine = rope_tables(positions, across, counts, offsets, HEAD_DIMENSION)
    return run(
        image_table.T, patches, ln_gain, ln_bias, merge_up.T, merge_up_bias, merge_down, merge_down_bias,
        text_embeds.T, attn_gain, q_weight, q_bias, key_value_weight, key_value_bias, o_weight, cosine, sine,
    )


def solution(mesh):
    return jax.shard_map(
        per_device,
        mesh=mesh,
        in_specs=(
            P(("seq", "tp"), None),
            P(),
            P(),
            P(),
            P(None, "tp"),
            P("tp"),
            P("tp", None),
            P(),
            P("seq", "tp"),
            P(),
            P(None, "tp"),
            P("tp"),
            P(),
            P(),
            P("tp", None),
        ),
        out_specs=P("seq", "tp"),
        check_vma=False,
    )
```

```python
import functools

import jax
import jax.numpy as jnp
import numpy as np
from jax import lax
from jax.experimental import pallas as pl
from jax.experimental.pallas import tpu as pltpu
from jax.sharding import PartitionSpec as P

MESH = pl.DeviceIdType.MESH
HEAD_DIMENSION = 128
KEY_VALUE_HEADS = 4
LOCAL_QUERY_HEAD = 16
CAP = 64
TOK_SEQ = 512
MW = 5120
VW = 1280
WIDTH = 3584
HID = 320
COLS = 224
N_TP = 16
N_SEQ = 8
SIDE = 4
ROWS = 448
HALF = 112
TCOL = 640
BLK = 896
RB = 128

EPS = 1e-06
THETA = 1000000.0
F32 = jnp.float32
BF16 = jnp.bfloat16


def al(value, multiple):
    return pl.multiple_of(value, multiple)


def place():
    t = lax.axis_index("tp")
    return t, t // SIDE, lax.rem(t, SIDE)


def wrap(value):
    return lax.rem(value + 2 * SIDE, SIDE)


def at_xy(x, y):
    return wrap(x) * SIDE + wrap(y)


def offset_xy(half, i, j):
    t, x, y = place()
    return (wrap(x + j), wrap(y + i)) if half == 0 else (wrap(x + i), wrap(y + j))


def peer(half, phase, sign):
    x, y = offset_xy(half, sign, 0) if phase == 1 else offset_xy(half, 0, sign)
    return x * SIDE + y


class Link:
    def __init__(self, send_sem, recv_sem, axis="tp"):
        self.send_sem, self.recv_sem, self.axis = send_sem, recv_sem, axis
        self.number, self.open = {}, []

    def _copy(self, key, src, dst, device):
        k = self.number.setdefault(key, len(self.number))
        return pltpu.make_async_remote_copy(
            src_ref=src,
            dst_ref=dst,
            send_sem=self.send_sem.at[k],
            recv_sem=self.recv_sem.at[k],
            device_id={self.axis: device},
            device_id_type=MESH,
        )

    def send(self, key, src, dst, device):
        copy = self._copy(key, src, dst, device)
        copy.start()
        self.open.append(copy)

    def arrived(self, key, dst, device):
        self._copy(key, dst, dst, device).wait_recv()

    def drain(self):
        assert len(self.number) <= self.send_sem.shape[0]
        for copy in self.open:
            copy.wait_send()
        self.open = []


def all_gather_2d(link, region, tag, own=None, hooks=(), lead=0):
    def reg(half, i, j, part):
        x, y = offset_xy(half, i, j)
        return region(half, x, y, part)

    def send(key, half, phase, sign, i, j, part):
        ref = reg(half, i, j, part)
        src = own(half) if own is not None and i == 0 and j == 0 else ref
        link.send((tag, half, *key), src, ref, peer(half, phase, sign))

    def got(key, half, phase, sign, i, j, part):
        link.arrived((tag, half, *key), reg(half, i, j, part), peer(half, phase, -sign))

    both = ((1, 0), (-1, 1))
    halves = (0, 1)

    def last(i, h):
        for s, part in both:
            got(("r2", s, i), h, 2, s, i, 2, part)

    for h in halves:
        for s, _ in both:
            send(("p1", s), h, 1, s, 0, 0, None)
    for h in halves:
        for s, _ in both:
            send(("p2", s, 0), h, 2, s, 0, 0, None)
    for s, part in both:
        for h in halves:
            got(("p1", s), h, 1, s, -s, 0, None)
            send(("r1", s), h, 1, s, -s, 0, part)
            for s2, _ in both:
                send(("p2", s2, -s), h, 2, s2, -s, 0, None)
    for s, part in both:
        for h in halves:
            got(("p2", s, 0), h, 2, s, 0, -s, None)
            send(("r2", s, 0), h, 2, s, 0, -s, part)
    for s, part in both:
        for h in halves:
            got(("r1", s), h, 1, s, 2, 0, part)
            for s2, _ in both:
                send(("p2", s2, 2, part), h, 2, s2, 2, 0, part)
    for i in (-1, 1):
        for s, part in both:
            for h in halves:
                got(("p2", s, i), h, 2, s, i, -s, None)
                send(("r2", s, i), h, 2, s, i, -s, part)
    last(0, lead)
    if hooks:
        hooks[0]()
    for s, part in both:
        for h in halves:
            got(("p2", s, 2, part), h, 2, s, 2, -s, part)
            send(("r2", s, 2), h, 2, s, 2, -s, part)
    for s, part in both:
        for h in halves:
            got(("p2", s, 2, 1 - part), h, 2, s, 2, -s, 1 - part)
    for n, i in enumerate((-1, 1)):
        last(i, lead)
        if hooks:
            hooks[1 + n]()
    last(2, lead)
    for i in (0, -1, 1, 2):
        last(i, 1 - lead)
    if hooks:
        hooks[3]()


AG_SEMS = 44


ORDER = (0, -1, 1, 2)
SIGNS = ((1, 0), (-1, 1))
HROW = RB // 2
QROW = RB // 4
D = HEAD_DIMENSION


def chosen(index, pieces):
    value = pieces[0]
    for k in range(1, len(pieces)):
        value = jnp.where(index == k, pieces[k], value)
    return value


def row_of(ref):
    return ref[...].reshape(1, ref.shape[0])


def layout(table, s):
    start, length, base = [], [], []
    so_far = 0
    for e in range(N_TP):
        i = 2 * N_TP * s + 2 * e
        first = (table[0, i] // 2) * (table[1, i] // 2)
        second = (table[0, i + 1] // 2) * (table[1, i + 1] // 2)
        start.append(table[2, i])
        length.append(first + second)
        base.append(so_far)
        so_far = so_far + first + second
    return start, length, base


def body(
    table, patches_hbm, ln_gain, ln_bias, up_hbm, up_bias, down_hbm, down_bias, text_hbm, gain, q_weight, q_bias,
    kv_weight, kv_bias, o_hbm, frequency, out,
    up, down, o_rows, o_send, o_cols, outgoing, incoming, tokens, lifted, hidden, pa, pb,
    a_raw, a_mid, a_out, a_sum, b_raw, b_mid, b_out, b_sum, c_raw, c_mid, c_out, shard,
    rows_ref, weight, normed, query, kv, heads, best, total, acc, pick_ref, cosine, sine, out_turned, out_sum, patches, text, load_sem, send_sem, recv_sem, seq_send, seq_recv,
):
    t, x, y = place()
    s = lax.axis_index("seq")
    z, core = s // 2, lax.rem(s, 2)

    def at(dz, dc):
        return lax.rem(z + dz + SIDE, SIDE) * 2 + lax.rem(core + dc, 2)

    barrier = pltpu.get_barrier_semaphore()
    for o in range(1, N_TP):
        pl.semaphore_signal(barrier, inc=1, device_id={"tp": lax.rem(t + o, N_TP)}, device_id_type=MESH)
    for device in (at(1, 0), at(-1, 0), at(0, 1)):
        pl.semaphore_signal(barrier, inc=1, device_id={"seq": device}, device_id_type=MESH)

    def load(n, src, dst):
        copy = pltpu.make_async_copy(src, dst, load_sem.at[n])
        copy.start()
        return copy

    load_patches = load(6, patches_hbm, patches)
    load_o = load(0, o_hbm.at[pl.ds(al(s * 16, 16), 16), :], o_rows)
    link = Link(send_sem, recv_sem)
    along = Link(seq_send, seq_recv, "seq")
    start, length, base = layout(table, s)

    load_patches.wait()
    value = patches[...].astype(F32)
    centre = jnp.mean(value, axis=-1, keepdims=True)
    centred = value - centre
    spread = jnp.mean(centred * centred, axis=-1, keepdims=True)
    fine = (centred * lax.rsqrt(spread + EPS) * row_of(ln_gain) + row_of(ln_bias)).astype(BF16)
    my_base, my_length = chosen(t, base), chosen(t, length)
    slot = lax.broadcasted_iota(jnp.int32, (CAP, 4 * CAP), 0)
    lane = lax.broadcasted_iota(jnp.int32, (CAP, 4 * CAP), 1)
    token = 2 * lax.rem(slot, 32) + lax.rem(slot // 32 + my_base, 2)
    source = jnp.where(token < my_length, 4 * token, -8)
    pl.semaphore_wait(barrier, N_TP + 2)
    for i in (1, 2, 3, 0):
        q = wrap(x + i)
        part = jnp.dot((lane == source + q).astype(BF16), fine, preferred_element_type=F32).astype(BF16)
        for u in range(2):
            for r in range(2):
                outgoing[4 * q + 2 * u + r] = part[r * 32 : (r + 1) * 32, u * TCOL : (u + 1) * TCOL]
        for j in (1, 2, 3, 0):
            if (i, j) != (0, 0):
                to = at_xy(x + i, y + j)
                link.send(("a", i, j), outgoing.at[to], incoming.at[t], to)
    incoming[t] = outgoing[t]

    load_o.wait()
    o_all = o_rows[...]
    for d in range(N_TP):
        o_send[d] = o_all[:, d * COLS : (d + 1) * COLS]
    o_place = pl.ds(al(s * 16, 16), 16)
    for o in range(1, N_TP):
        to = lax.rem(t + o, N_TP)
        link.send(("o", o), o_send.at[to], o_cols.at[t, o_place, :], to)
    o_cols[t, o_place, :] = o_send[t]

    load_up = load(1, up_hbm, up)
    load_down = load(2, down_hbm, down)
    load_text = load(7, text_hbm, text)
    load_qkv = [
        load(3, q_weight, weight.at[:, pl.ds(0, D)]),
        load(4, kv_weight.at[:, pl.ds(al(x * D, 128), D)], weight.at[:, pl.ds(D, D)]),
        load(5, kv_weight.at[:, pl.ds(al((KEY_VALUE_HEADS + x) * D, 128), D)], weight.at[:, pl.ds(2 * D, D)]),
    ]

    half_of = lax.rem(t, 2)
    lane = lax.broadcasted_iota(jnp.int32, (1, N_TP * 32), 1)
    base_row = jnp.zeros((1, N_TP * 32), jnp.int32)
    length_row = base_row
    for e in range(N_TP):
        here = lane // 32 == e
        base_row = jnp.where(here, base[e], base_row)
        length_row = jnp.where(here, length[e], length_row)
    taken = 2 * lax.rem(lane, 32) + lax.rem(half_of + base_row, 2)
    target = jnp.where(taken < length_row, (base_row + taken) // 2, -1)
    pick = (lax.broadcasted_iota(jnp.int32, (2 * HALF, N_TP * 32), 0) == target).astype(BF16)
    for i in (1, 2, 3, 0):
        for j in (1, 2, 3, 0):
            if (i, j) != (0, 0):
                frm = at_xy(x - i, y - j)
                link.arrived(("a", i, j), incoming.at[frm], frm)
    slots = incoming[...].reshape(N_TP * 32, TCOL)
    mine = jnp.dot(pick, slots, preferred_element_type=F32).astype(BF16)
    tokens[pl.ds(al(half_of * 2 * HALF, 2 * HALF), 2 * HALF), pl.ds(al(t // 2 * TCOL, 128), TCOL)] = mine

    def token_region(half, x, y, part):
        d = x * SIDE + y
        first, width = ((0, TCOL), (0, 384), (384, 256))[0 if part is None else 1 + part]
        return tokens.at[
            pl.ds(al(lax.rem(d, 2) * 2 * HALF + half * HALF, 16), HALF),
            pl.ds(al(d // 2 * TCOL + first, 128), width),
        ]

    def o_region(dz, dc, part):
        first, count = ((0, N_TP), (0, 8), (8, 8))[0 if part is None else 1 + part]
        return o_cols.at[pl.ds(first, count), pl.ds(al(at(dz, dc) * 16, 16), 16), :]

    spot = (
        lax.broadcasted_iota(jnp.int32, (COLS, BLK), 0) + y * COLS == lax.broadcasted_iota(jnp.int32, (COLS, BLK), 1)
    ).astype(BF16)
    own = pl.ds(al(x * BLK, 128), BLK)
    at_lane = s * TOK_SEQ + lax.broadcasted_iota(jnp.int32, (1, TOK_SEQ), 1)

    def find_rows():
        order = lax.broadcasted_iota(jnp.int32, (TOK_SEQ, 1), 0)
        pos = s * TOK_SEQ + lax.rem(order, 256) // HROW * RB + order // 256 * HROW + lax.rem(order, HROW)
        where = jnp.full((TOK_SEQ, 1), -1, jnp.int32)
        for e in range(N_TP):
            inner = pos - start[e]
            where = jnp.where((inner >= 0) & (inner < length[e]), base[e] + inner, where)
        where = jnp.where(where >= 0, lax.rem(where, 2) * 2 * HALF + where // 2, -1)
        pick_ref[...] = (lax.broadcasted_iota(jnp.int32, (TOK_SEQ, ROWS), 1) == where).astype(BF16)

    def find_words():
        load_text.wait()
        plain = jnp.ones((1, TOK_SEQ), F32)
        for e in range(N_TP):
            plain = jnp.where((at_lane >= start[e]) & (at_lane < start[e] + length[e]), 0.0, plain)
        words = (text[...].astype(F32) * plain).astype(BF16)
        for rb in range(SIDE):
            add = lax.dot_general(
                words[:, rb * RB : (rb + 1) * RB], spot, (((0,), (0,)), ((), ())), preferred_element_type=F32
            ).astype(BF16)
            a_sum[rb] = add[:HROW]
            b_sum[:, rb * BLK : (rb + 1) * BLK] = add[HROW:]

    def find_angles():
        run, across = at_lane, jnp.ones((1, TOK_SEQ), jnp.int32)
        for i in range(2 * N_TP):
            k = 2 * N_TP * s + i
            first, width = table[2, k], table[1, k] // 2
            inside = (at_lane >= first) & (at_lane < first + (table[0, k] // 2) * width)
            run = jnp.where(inside, first, run)
            across = jnp.where(inside, width, across)
        inner = (at_lane - run).astype(F32)
        wide = across.astype(F32)
        line = jnp.floor((inner + 0.5) / wide)
        begin = run.astype(F32)
        stack = jnp.concatenate(
            [begin, begin + line, begin + (inner - line * wide), jnp.zeros((5, TOK_SEQ), F32)], axis=0
        )
        turned = jnp.transpose(stack)
        f = lax.rem(lax.broadcasted_iota(jnp.int32, (1, D), 1), D // 2)
        position = jnp.where(f < 16, turned[:, 0:1], jnp.where(f < 40, turned[:, 1:2], turned[:, 2:3]))
        angle = position * frequency[...]
        cosine[...] = jnp.cos(angle)
        lane = lax.broadcasted_iota(jnp.int32, (1, D), 1)
        sine[...] = jnp.sin(angle) * jnp.where(lane < D // 2, -1.0, 1.0)

    def lift(n):
        cols = pl.ds(al(wrap(x + ORDER[n]) * VW, 128), VW)
        got = lax.dot_general(
            tokens[:, cols], up[:, cols], (((1,), (1,)), ((), ())), preferred_element_type=F32
        )
        if n == 0:
            lifted[...] = got + row_of(up_bias)
        else:
            lifted[...] += got

    def lift_first():
        load_up.wait()
        lift(0)
        for o in range(1, N_TP):
            frm = lax.rem(t - o + N_TP, N_TP)
            link.arrived(("o", o), o_cols.at[frm, o_place, :], frm)
        for sg, _ in SIGNS:
            along.send(("o", "z", sg), o_region(0, 0, None), o_region(0, 0, None), at(sg, 0))
        along.send(("o", "c", 0), o_region(0, 0, None), o_region(0, 0, None), at(0, 1))
        find_rows()

    def lift_second():
        lift(1)
        find_angles()

    def lift_third():
        lift(2)
        find_words()

    all_gather_2d(
        link, token_region, "t", None, (lift_first, lift_second, lift_third, functools.partial(lift, 3)), 1
    )

    raised = lifted[...]
    act = (0.5 * raised * (1.0 + lax.erf(raised * 0.5**0.5))).astype(BF16)
    hidden[...] = jnp.dot(pick_ref[...], act, preferred_element_type=F32).astype(BF16)
    load_down.wait()
    def lower_a(i):
        cols = pl.ds(al(wrap(x + i) * BLK, 128), BLK)
        got = jnp.dot(hidden[0:256, :], down[:, cols], preferred_element_type=F32)
        pa[:, :, cols] = got.astype(BF16).reshape(SIDE, HROW, BLK)

    def a_piece(i, part):
        rows = (pl.ds(0, SIDE), pl.ds(0, 2), pl.ds(2, 2))[0 if part is None else 1 + part]
        return pa.at[rows, :, pl.ds(al(wrap(x + i) * BLK, 128), BLK)]

    def b_piece(i, part):
        cols = (pl.ds(0, WIDTH), pl.ds(0, WIDTH // 2), pl.ds(WIDTH // 2, WIDTH // 2))[0 if part is None else 1 + part]
        return pb.at[wrap(y + i), :, cols]

    def to_x(sg):
        return at_xy(x + sg, y)

    def to_y(sg):
        return at_xy(x, y + sg)

    def mid_of(ref, name, part):
        if name == "a":
            return ref.at[pl.ds(2 * part, 2)]
        return ref.at[:, pl.ds(part * (WIDTH // 2), WIDTH // 2)]

    def make_a(i):
        lower_a(i)
        if i == 0:
            pa[:, :, own] = (pa[:, :, own].astype(F32) + a_sum[...].astype(F32)).astype(BF16)

    def make_b():
        for c in range(SIDE):
            cols = slice(c * BLK, (c + 1) * BLK)
            got = jnp.dot(hidden[256:, :], down[:, cols], preferred_element_type=F32)
            pb[:, :, cols] = got.astype(BF16).reshape(SIDE, HROW, BLK)
        for rb in range(SIDE):
            add = b_sum[:, rb * BLK : (rb + 1) * BLK].astype(F32)
            pb[rb, :, own] = (pb[rb, :, own].astype(F32) + add).astype(BF16)

    sides = (("a", a_piece, a_raw, a_mid, a_out, to_x), ("b", b_piece, b_raw, b_mid, b_out, to_y))

    def send_raw(n, piece, raw, mid, outb, to):
        for sg, part in SIGNS:
            link.send((n, "raw", sg), piece(2, part), raw.at[part], to(sg))

    def send_own(sg, part, n, piece, raw, mid, outb, to):
        link.send((n, "own", sg), piece(sg, 1 - part), mid_of(mid.at[part], n, 1 - part), to(sg))

    make_a(2)
    send_raw(*sides[0])
    make_b()
    send_raw(*sides[1])
    for sg, part in SIGNS:
        send_own(sg, part, *sides[1])
    for sg, part in SIGNS:
        make_a(sg)
        send_own(sg, part, *sides[0])
    for n, piece, raw, mid, outb, to in sides:
        for sg, part in SIGNS:
            link.arrived((n, "raw", sg), raw.at[part], to(-sg))
            outb[part] = (raw[part].astype(F32) + piece(sg, part)[...].astype(F32)).astype(BF16)
            link.send((n, "sum", sg), outb.at[part], mid_of(mid.at[part], n, part), to(sg))
    make_a(0)

    for sg, part in SIGNS:
        along.arrived(("o", "z", sg), o_region(-sg, 0, None), at(-sg, 0))
        along.send(("o", "r", sg), o_region(-sg, 0, part), o_region(-sg, 0, part), at(sg, 0))
        along.send(("o", "c", -sg), o_region(-sg, 0, None), o_region(-sg, 0, None), at(0, 1))

    def a_next(i, part):
        rows = (pl.ds(0, HROW), pl.ds(0, QROW), pl.ds(QROW, QROW))[0 if part is None else 1 + part]
        return a_sum.at[wrap(y + i), rows, :]

    def b_next(i, part):
        rows = (pl.ds(0, HROW), pl.ds(0, QROW), pl.ds(QROW, QROW))[0 if part is None else 1 + part]
        return b_sum.at[rows, pl.ds(al(wrap(x + i) * BLK, 128), BLK)]

    after = ((0, a_next, to_y), (1, b_next, to_x))
    for side, nxt in zip(sides, after):
        n, piece, raw, mid, outb, to = side
        for sg, part in SIGNS:
            link.arrived((n, "own", sg), mid_of(mid.at[part], n, 1 - part), to(-sg))
            link.arrived((n, "sum", sg), mid_of(mid.at[part], n, part), to(-sg))
        held = a_sum if n == "a" else b_sum
        held[...] = (piece(0, None)[...].astype(F32) + mid[0].astype(F32) + mid[1].astype(F32)).astype(BF16)
        n, piece, to = nxt
        for sg, part in SIGNS:
            link.send((n, "raw2", sg), piece(2, part), c_raw.at[n, part], to(sg))
        for sg, part in SIGNS:
            link.send((n, "own2", sg), piece(sg, 1 - part), c_mid.at[n, part, 1 - part], to(sg))
    for n, piece, to in after:
        for sg, part in SIGNS:
            link.arrived((n, "raw2", sg), c_raw.at[n, part], to(-sg))
            c_out[n, part] = (c_raw[n, part].astype(F32) + piece(sg, part)[...].astype(F32)).astype(BF16)
            link.send((n, "sum2", sg), c_out.at[n, part], c_mid.at[n, part, part], to(sg))
    row = s * TOK_SEQ + y * RB + lax.broadcasted_iota(jnp.int32, (RB, 1), 0)
    image = jnp.zeros((RB, 1), F32)
    for e in range(N_TP):
        image = jnp.where((row >= start[e]) & (row < start[e] + length[e]), 1.0, image)
    full_bias = row_of(down_bias)
    shift = image * chosen(x, [full_bias[:, k * BLK : (k + 1) * BLK] for k in range(SIDE)])
    for n, piece, to in after:
        for sg, part in SIGNS:
            link.arrived((n, "own2", sg), c_mid.at[n, part, 1 - part], to(-sg))
            link.arrived((n, "sum2", sg), c_mid.at[n, part, part], to(-sg))
        held = piece(0, None)[...].astype(F32)
        held = held + c_mid[n, 0].reshape(HROW, BLK).astype(F32) + c_mid[n, 1].reshape(HROW, BLK).astype(F32)
        shard[pl.ds(n * HROW, HROW), :] = (held + shift[n * HROW : (n + 1) * HROW]).astype(BF16)

    for sg, part in SIGNS:
        along.arrived(("o", "r", sg), o_region(2, 0, part), at(-sg, 0))
        along.send(("o", "c", 2, part), o_region(2, 0, part), o_region(2, 0, part), at(0, 1))

    def region(half, x, y, part):
        first, count = ((0, HROW), (0, QROW), (QROW, QROW))[0 if part is None else 1 + part]
        return rows_ref.at[
            pl.ds(al(y * RB + half * HROW + first, QROW), count),
            pl.ds(al(x * BLK, 128), BLK),
        ]

    def kv_at(n, dz, dc):
        return kv.at[at(dz, dc), pl.ds(al(wrap(y + ORDER[n]) * RB, RB), RB), :]

    kv_row = row_of(kv_bias)
    heads_of = [kv_row[:, k * D : (k + 1) * D] for k in range(2 * KEY_VALUE_HEADS)]
    key_bias, value_bias = chosen(x, heads_of[:KEY_VALUE_HEADS]), chosen(x, heads_of[KEY_VALUE_HEADS:])

    def project(n):
        rows = pl.ds(al(wrap(y + ORDER[n]) * RB, RB), RB)
        value = rows_ref[rows, :].astype(F32)
        scale = lax.rsqrt(jnp.mean(value * value, axis=-1, keepdims=True) + EPS)
        normed[...] = (value * scale * row_of(gain)).astype(BF16)
        got = jnp.dot(normed[...], weight[...], preferred_element_type=F32)
        c, sn = cosine[rows, :], sine[rows, :]
        q, k = got[:, :D] + row_of(q_bias), got[:, D : 2 * D] + key_bias
        kv[s, rows, 0:D] = (k * c + pltpu.roll(k, D // 2, 1) * sn).astype(BF16)
        kv[s, rows, D : 2 * D] = (got[:, 2 * D :] + value_bias).astype(BF16)
        for sg, _ in SIGNS:
            along.send((n, "z", sg), kv_at(n, 0, 0), kv_at(n, 0, 0), at(sg, 0))
        along.send((n, "z", 2), kv_at(n, 0, 0), kv_at(n, 0, 0), at(2, 0))
        along.send((n, "c", 0), kv_at(n, 0, 0), kv_at(n, 0, 0), at(0, 1))
        query[rows, :] = (q * c + pltpu.roll(q, D // 2, 1) * sn).astype(BF16)

    def relay(n, steps):
        for dz in steps:
            along.arrived((n, "z", -dz if dz != 2 else 2), kv_at(n, dz, 0), at(dz, 0))
            along.send((n, "c", dz), kv_at(n, dz, 0), kv_at(n, dz, 0), at(0, 1))

    def first():
        for copy in load_qkv:
            copy.wait()
        project(0)

    def third():
        project(2)
        relay(0, (-1, 1, 2))

    def fourth():
        relay(1, (-1, 1, 2))
        project(3)
        relay(2, (-1, 1, 2))

    rows_ref[pl.ds(al(y * RB, RB), RB), own] = shard[...]
    all_gather_2d(
        link, region, "x", lambda half: shard.at[pl.ds(half * HROW, HROW)],
        (first, functools.partial(project, 1), third, fourth),
    )

    step = HEAD_DIMENSION ** (-0.5)
    chunk = 256

    def attend(b, causal):
        keys, values = kv[b, :, 0:D], kv[b, :, D : 2 * D]
        for r in range(TOK_SEQ // chunk):
            rows = slice(r * chunk, (r + 1) * chunk)
            width = (r + 1) * chunk if causal else TOK_SEQ
            score = lax.dot_general(query[rows, :], keys[:width], (((1,), (1,)), ((), ())), preferred_element_type=F32)
            if causal:
                down_row = lax.broadcasted_iota(jnp.int32, score.shape, 0) + r * chunk
                col = lax.broadcasted_iota(jnp.int32, score.shape, 1)
                score = jnp.where(col <= down_row, score, -1e30)
                top = jnp.max(score, axis=1, keepdims=True)
                p = jnp.exp((score - top) * step)
                total[rows, :] = jnp.sum(p, axis=1, keepdims=True)
                acc[rows, :] = jnp.dot(p.astype(BF16), values[:width], preferred_element_type=F32)
            else:
                old = best[rows, :]
                top = jnp.maximum(old, jnp.max(score, axis=1, keepdims=True))
                fade = jnp.exp((old - top) * step)
                p = jnp.exp((score - top) * step)
                total[rows, :] = total[rows, :] * fade + jnp.sum(p, axis=1, keepdims=True)
                acc[rows, :] = acc[rows, :] * fade + jnp.dot(p.astype(BF16), values, preferred_element_type=F32)
            best[rows, :] = top

    def attend_if(dz, dc):
        b = at(dz, dc)

        @pl.when(b < s)
        def _():
            attend(b, False)

    attend(s, True)
    relay(3, (-1, 1))
    for n in range(4):
        along.arrived((n, "c", 0), kv_at(n, 0, 1), at(0, 1))
    attend_if(0, 1)
    relay(3, (2,))
    for dz in (-1, 1, 2):
        attend_if(dz, 0)
        for n in range(4):
            along.arrived((n, "c", dz), kv_at(n, dz, 1), at(0, 1))
        attend_if(dz, 1)
    heads[:, pl.ds(al(t * D, 128), D)] = (acc[...] / total[...]).astype(BF16)

    def head_region(half, x, y, part):
        first, count = ((0, 256), (0, 128), (128, 128))[0 if part is None else 1 + part]
        return heads.at[pl.ds(half * 256 + first, count), pl.ds(al((x * SIDE + y) * D, 128), D)]

    def mix(n):
        if n == 0:
            for dz in (0, -1, 1):
                along.arrived(("o", "c", dz), o_region(dz, 1, None), at(0, 1))
            for part in (0, 1):
                along.arrived(("o", "c", 2, part), o_region(2, 1, part), at(0, 1))
            out_turned[...] = jnp.transpose(o_cols[...].reshape(LOCAL_QUERY_HEAD * D, COLS))
            out_sum[...] = lax.dot_general(
                spot, rows_ref[:, own], (((1,), (1,)), ((), ())), preferred_element_type=F32
            )
        cols = pl.ds(al(wrap(x + ORDER[n]) * SIDE * D, 128), SIDE * D)
        got = lax.dot_general(
            out_turned[:, cols], heads[:, cols], (((1,), (1,)), ((), ())), preferred_element_type=F32
        )
        if n < 3:
            out_sum[...] += got
        else:
            out[...] = (out_sum[...] + got).astype(BF16)

    all_gather_2d(link, head_region, "h", None, [functools.partial(mix, n) for n in range(4)], 1)
    link.drain()
    along.drain()


LINKS = 3 * AG_SEMS + 30 + 24
ALONG = 9 + 28


def run(*operands):
    vmem = pl.BlockSpec(memory_space=pltpu.VMEM)
    hbm = pl.BlockSpec(memory_space=pl.ANY)
    smem = pl.BlockSpec(memory_space=pltpu.SMEM)

    def b16(*shape):
        return pltpu.VMEM(shape, BF16)

    def f32(*shape):
        return pltpu.VMEM(shape, F32)

    return pl.pallas_call(
        body,
        out_shape=jax.ShapeDtypeStruct((COLS, TOK_SEQ), BF16),
        in_specs=[
            smem, hbm, vmem, vmem, hbm, vmem, hbm, vmem, hbm, vmem, hbm, vmem, hbm, vmem, hbm, vmem
        ],
        out_specs=vmem,
        scratch_shapes=[
            b16(HID, MW), b16(HID, WIDTH), b16(16, WIDTH), b16(N_TP, 16, COLS), b16(N_TP, D, COLS),
            b16(N_TP, 32, TCOL), b16(N_TP, 32, TCOL), b16(ROWS, MW), f32(ROWS, HID), b16(TOK_SEQ, HID),
            b16(SIDE, HROW, WIDTH), b16(SIDE, HROW, WIDTH),
            b16(2, 2, HROW, BLK), b16(2, SIDE, HROW, BLK), b16(2, 2, HROW, BLK), b16(SIDE, HROW, BLK),
            b16(2, HROW, WIDTH // 2), b16(2, HROW, WIDTH), b16(2, HROW, WIDTH // 2), b16(HROW, WIDTH),
            b16(2, 2, QROW, BLK), b16(2, 2, 2, QROW, BLK), b16(2, 2, QROW, BLK), b16(RB, BLK),
            b16(TOK_SEQ, WIDTH), b16(WIDTH, 3 * D), b16(RB, WIDTH), b16(TOK_SEQ, D), b16(N_SEQ, TOK_SEQ, 2 * D),
            b16(TOK_SEQ, LOCAL_QUERY_HEAD * D), f32(TOK_SEQ, 1), f32(TOK_SEQ, 1), f32(TOK_SEQ, D),
            b16(TOK_SEQ, ROWS), f32(TOK_SEQ, D), f32(TOK_SEQ, D), b16(COLS, LOCAL_QUERY_HEAD * D), f32(COLS, TOK_SEQ),
            b16(4 * CAP, VW), b16(COLS, TOK_SEQ),
            pltpu.SemaphoreType.DMA((8,)),
            pltpu.SemaphoreType.DMA((LINKS,)), pltpu.SemaphoreType.DMA((LINKS,)),
            pltpu.SemaphoreType.DMA((ALONG,)), pltpu.SemaphoreType.DMA((ALONG,)),
        ],
        compiler_params=pltpu.CompilerParams(
            collective_id=0, has_side_effects=True, vmem_limit_bytes=60 * 1024 * 1024
        ),
        name="block",
    )(*operands)


def per_device(
    patches, image_table, ln_gain, ln_bias, merge_up, merge_up_bias, merge_down, merge_down_bias,
    text_embeds, attn_gain, q_weight, q_bias, key_value_weight, key_value_bias, o_weight,
):
    half = D // 2
    powers = np.float32(THETA) ** (np.float32(-2.0) * np.arange(half, dtype=np.float32) / np.float32(D))
    frequency = jnp.asarray(np.concatenate([powers, powers]).astype(np.float32).reshape(1, D))
    return run(
        image_table.T, patches, ln_gain, ln_bias, merge_up.T, merge_up_bias, merge_down, merge_down_bias,
        text_embeds.T, attn_gain, q_weight, q_bias, key_value_weight, key_value_bias, o_weight, frequency,
    ).T


def solution(mesh):
    return jax.shard_map(
        per_device,
        mesh=mesh,
        in_specs=(
            P(("seq", "tp"), None),
            P(),
            P(),
            P(),
            P(None, "tp"),
            P("tp"),
            P("tp", None),
            P(),
            P("seq", "tp"),
            P(),
            P(None, "tp"),
            P("tp"),
            P(),
            P(),
            P("tp", None),
        ),
        out_specs=P("seq", "tp"),
        check_vma=False,
    )
```

```python
import functools

import jax
import jax.numpy as jnp
import numpy as np
from jax import lax
from jax.experimental import pallas as pl
from jax.experimental.pallas import tpu as pltpu
from jax.sharding import PartitionSpec as P

MESH = pl.DeviceIdType.MESH
HEAD_DIMENSION = 128
KEY_VALUE_HEADS = 4
LOCAL_QUERY_HEAD = 16
CAP = 64
TOK_SEQ = 512
MW = 5120
VW = 1280
WIDTH = 3584
HID = 320
COLS = 224
N_TP = 16
N_SEQ = 8
SIDE = 4
ROWS = 448
HALF = 112
TCOL = 640
BLK = 896
RB = 128

EPS = 1e-06
THETA = 1000000.0
F32 = jnp.float32
BF16 = jnp.bfloat16


def al(value, multiple):
    return pl.multiple_of(value, multiple)


def place():
    t = lax.axis_index("tp")
    return t, t // SIDE, lax.rem(t, SIDE)


def wrap(value):
    return lax.rem(value + 2 * SIDE, SIDE)


def at_xy(x, y):
    return wrap(x) * SIDE + wrap(y)


def offset_xy(half, i, j):
    t, x, y = place()
    return (wrap(x + j), wrap(y + i)) if half == 0 else (wrap(x + i), wrap(y + j))


def peer(half, phase, sign):
    x, y = offset_xy(half, sign, 0) if phase == 1 else offset_xy(half, 0, sign)
    return x * SIDE + y


class Link:
    def __init__(self, send_sem, recv_sem, axis="tp"):
        self.send_sem, self.recv_sem, self.axis = send_sem, recv_sem, axis
        self.number, self.open = {}, []

    def _copy(self, key, src, dst, device):
        k = self.number.setdefault(key, len(self.number))
        return pltpu.make_async_remote_copy(
            src_ref=src,
            dst_ref=dst,
            send_sem=self.send_sem.at[k],
            recv_sem=self.recv_sem.at[k],
            device_id={self.axis: device},
            device_id_type=MESH,
        )

    def send(self, key, src, dst, device):
        copy = self._copy(key, src, dst, device)
        copy.start()
        self.open.append(copy)

    def arrived(self, key, dst, device):
        self._copy(key, dst, dst, device).wait_recv()

    def drain(self):
        assert len(self.number) <= self.send_sem.shape[0]
        for copy in self.open:
            copy.wait_send()
        self.open = []


def all_gather_2d(link, region, tag, own=None, hooks=(), lead=0):
    def reg(half, i, j, part):
        x, y = offset_xy(half, i, j)
        return region(half, x, y, part)

    def send(key, half, phase, sign, i, j, part):
        ref = reg(half, i, j, part)
        src = own(half) if own is not None and i == 0 and j == 0 else ref
        link.send((tag, half, *key), src, ref, peer(half, phase, sign))

    def got(key, half, phase, sign, i, j, part):
        link.arrived((tag, half, *key), reg(half, i, j, part), peer(half, phase, -sign))

    both = ((1, 0), (-1, 1))
    halves = (0, 1)

    def last(i, h):
        for s, part in both:
            got(("r2", s, i), h, 2, s, i, 2, part)

    for h in halves:
        for s, _ in both:
            send(("p1", s), h, 1, s, 0, 0, None)
    for h in halves:
        for s, _ in both:
            send(("p2", s, 0), h, 2, s, 0, 0, None)
    for s, part in both:
        for h in halves:
            got(("p1", s), h, 1, s, -s, 0, None)
            send(("r1", s), h, 1, s, -s, 0, part)
            for s2, _ in both:
                send(("p2", s2, -s), h, 2, s2, -s, 0, None)
    for s, part in both:
        for h in halves:
            got(("p2", s, 0), h, 2, s, 0, -s, None)
            send(("r2", s, 0), h, 2, s, 0, -s, part)
    for s, part in both:
        for h in halves:
            got(("r1", s), h, 1, s, 2, 0, part)
            for s2, _ in both:
                send(("p2", s2, 2, part), h, 2, s2, 2, 0, part)
    for i in (-1, 1):
        for s, part in both:
            for h in halves:
                got(("p2", s, i), h, 2, s, i, -s, None)
                send(("r2", s, i), h, 2, s, i, -s, part)
    last(0, lead)
    if hooks:
        hooks[0]()
    for s, part in both:
        for h in halves:
            got(("p2", s, 2, part), h, 2, s, 2, -s, part)
            send(("r2", s, 2), h, 2, s, 2, -s, part)
    for s, part in both:
        for h in halves:
            got(("p2", s, 2, 1 - part), h, 2, s, 2, -s, 1 - part)
    for n, i in enumerate((-1, 1)):
        last(i, lead)
        if hooks:
            hooks[1 + n]()
    last(2, lead)
    for i in (0, -1, 1, 2):
        last(i, 1 - lead)
    if hooks:
        hooks[3]()


AG_SEMS = 44


ORDER = (0, -1, 1, 2)
SIGNS = ((1, 0), (-1, 1))
DIRECT = ((2, 2), (1, 0), (-1, 1))
HROW = RB // 2
QROW = RB // 4
D = HEAD_DIMENSION


def chosen(index, pieces):
    value = pieces[0]
    for k in range(1, len(pieces)):
        value = jnp.where(index == k, pieces[k], value)
    return value


def row_of(ref):
    return ref[...].reshape(1, ref.shape[0])


def layout(table, s):
    start, length, base = [], [], []
    so_far = 0
    for e in range(N_TP):
        i = 2 * N_TP * s + 2 * e
        first = (table[0, i] // 2) * (table[1, i] // 2)
        second = (table[0, i + 1] // 2) * (table[1, i + 1] // 2)
        start.append(table[2, i])
        length.append(first + second)
        base.append(so_far)
        so_far = so_far + first + second
    return start, length, base


def body(
    table, patches_hbm, ln_gain, ln_bias, up_hbm, up_bias, down_hbm, down_bias, text_hbm, gain, q_weight, q_bias,
    kv_weight, kv_bias, o_hbm, frequency, out,
    up, down, o_rows, o_send, o_cols, outgoing, incoming, tokens, lifted, hidden, pa, pb,
    a_raw, a_mid, a_out, a_sum, b_raw, b_mid, b_out, b_sum, c_mid, shard,
    rows_ref, weight, normed, query, kv, heads, best, total, acc, pick_ref, cosine, sine, out_turned, out_sum, patches, text, load_sem, send_sem, recv_sem, seq_send, seq_recv,
):
    t, x, y = place()
    s = lax.axis_index("seq")
    z, core = s // 2, lax.rem(s, 2)

    def at(dz, dc):
        return lax.rem(z + dz + SIDE, SIDE) * 2 + lax.rem(core + dc, 2)

    barrier = pltpu.get_barrier_semaphore()
    for o in range(1, N_TP):
        pl.semaphore_signal(barrier, inc=1, device_id={"tp": lax.rem(t + o, N_TP)}, device_id_type=MESH)
    for device in (at(1, 0), at(-1, 0), at(0, 1)):
        pl.semaphore_signal(barrier, inc=1, device_id={"seq": device}, device_id_type=MESH)

    def load(n, src, dst):
        copy = pltpu.make_async_copy(src, dst, load_sem.at[n])
        copy.start()
        return copy

    load_patches = load(6, patches_hbm, patches)
    load_o = load(0, o_hbm.at[pl.ds(al(s * 16, 16), 16), :], o_rows)
    link = Link(send_sem, recv_sem)
    along = Link(seq_send, seq_recv, "seq")
    start, length, base = layout(table, s)

    load_patches.wait()
    value = patches[...].astype(F32)
    centre = jnp.mean(value, axis=-1, keepdims=True)
    centred = value - centre
    spread = jnp.mean(centred * centred, axis=-1, keepdims=True)
    fine = (centred * lax.rsqrt(spread + EPS) * row_of(ln_gain) + row_of(ln_bias)).astype(BF16)
    my_base, my_length = chosen(t, base), chosen(t, length)
    slot = lax.broadcasted_iota(jnp.int32, (CAP, 4 * CAP), 0)
    lane = lax.broadcasted_iota(jnp.int32, (CAP, 4 * CAP), 1)
    token = 2 * lax.rem(slot, 32) + lax.rem(slot // 32 + my_base, 2)
    source = jnp.where(token < my_length, 4 * token, -8)
    pl.semaphore_wait(barrier, N_TP + 2)
    for i in (1, 2, 3, 0):
        q = wrap(x + i)
        part = jnp.dot((lane == source + q).astype(BF16), fine, preferred_element_type=F32).astype(BF16)
        for u in range(2):
            for r in range(2):
                outgoing[4 * q + 2 * u + r] = part[r * 32 : (r + 1) * 32, u * TCOL : (u + 1) * TCOL]
        for j in (1, 2, 3, 0):
            if (i, j) != (0, 0):
                to = at_xy(x + i, y + j)
                link.send(("a", i, j), outgoing.at[to], incoming.at[t], to)
    incoming[t] = outgoing[t]

    load_o.wait()
    o_all = o_rows[...]
    for d in range(N_TP):
        o_send[d] = o_all[:, d * COLS : (d + 1) * COLS]
    o_place = pl.ds(al(s * 16, 16), 16)
    for o in range(1, N_TP):
        to = lax.rem(t + o, N_TP)
        link.send(("o", o), o_send.at[to], o_cols.at[t, o_place, :], to)
    o_cols[t, o_place, :] = o_send[t]

    load_up = load(1, up_hbm, up)
    load_down = load(2, down_hbm, down)
    load_text = load(7, text_hbm, text)
    load_qkv = [
        load(3, q_weight, weight.at[:, pl.ds(0, D)]),
        load(4, kv_weight.at[:, pl.ds(al(x * D, 128), D)], weight.at[:, pl.ds(D, D)]),
        load(5, kv_weight.at[:, pl.ds(al((KEY_VALUE_HEADS + x) * D, 128), D)], weight.at[:, pl.ds(2 * D, D)]),
    ]

    half_of = lax.rem(t, 2)
    lane = lax.broadcasted_iota(jnp.int32, (1, N_TP * 32), 1)
    base_row = jnp.zeros((1, N_TP * 32), jnp.int32)
    length_row = base_row
    for e in range(N_TP):
        here = lane // 32 == e
        base_row = jnp.where(here, base[e], base_row)
        length_row = jnp.where(here, length[e], length_row)
    taken = 2 * lax.rem(lane, 32) + lax.rem(half_of + base_row, 2)
    target = jnp.where(taken < length_row, (base_row + taken) // 2, -1)
    pick = (lax.broadcasted_iota(jnp.int32, (2 * HALF, N_TP * 32), 0) == target).astype(BF16)
    for i in (1, 2, 3, 0):
        for j in (1, 2, 3, 0):
            if (i, j) != (0, 0):
                frm = at_xy(x - i, y - j)
                link.arrived(("a", i, j), incoming.at[frm], frm)
    slots = incoming[...].reshape(N_TP * 32, TCOL)
    mine = jnp.dot(pick, slots, preferred_element_type=F32).astype(BF16)
    tokens[pl.ds(al(half_of * 2 * HALF, 2 * HALF), 2 * HALF), pl.ds(al(t // 2 * TCOL, 128), TCOL)] = mine

    def token_region(half, x, y, part):
        d = x * SIDE + y
        first, width = ((0, TCOL), (0, 384), (384, 256))[0 if part is None else 1 + part]
        return tokens.at[
            pl.ds(al(lax.rem(d, 2) * 2 * HALF + half * HALF, 16), HALF),
            pl.ds(al(d // 2 * TCOL + first, 128), width),
        ]

    def o_region(dz, dc, part):
        first, count = ((0, N_TP), (0, 8), (8, 8))[0 if part is None else 1 + part]
        return o_cols.at[pl.ds(first, count), pl.ds(al(at(dz, dc) * 16, 16), 16), :]

    spot = (
        lax.broadcasted_iota(jnp.int32, (COLS, BLK), 0) + y * COLS == lax.broadcasted_iota(jnp.int32, (COLS, BLK), 1)
    ).astype(BF16)
    own = pl.ds(al(x * BLK, 128), BLK)
    at_lane = s * TOK_SEQ + lax.broadcasted_iota(jnp.int32, (1, TOK_SEQ), 1)

    def find_rows():
        order = lax.broadcasted_iota(jnp.int32, (TOK_SEQ, 1), 0)
        pos = s * TOK_SEQ + lax.rem(order, 256) // HROW * RB + order // 256 * HROW + lax.rem(order, HROW)
        where = jnp.full((TOK_SEQ, 1), -1, jnp.int32)
        for e in range(N_TP):
            inner = pos - start[e]
            where = jnp.where((inner >= 0) & (inner < length[e]), base[e] + inner, where)
        where = jnp.where(where >= 0, lax.rem(where, 2) * 2 * HALF + where // 2, -1)
        pick_ref[...] = (lax.broadcasted_iota(jnp.int32, (TOK_SEQ, ROWS), 1) == where).astype(BF16)

    def find_words():
        load_text.wait()
        plain = jnp.ones((1, TOK_SEQ), F32)
        for e in range(N_TP):
            plain = jnp.where((at_lane >= start[e]) & (at_lane < start[e] + length[e]), 0.0, plain)
        words = (text[...].astype(F32) * plain).astype(BF16)
        for rb in range(SIDE):
            add = lax.dot_general(
                words[:, rb * RB : (rb + 1) * RB], spot, (((0,), (0,)), ((), ())), preferred_element_type=F32
            ).astype(BF16)
            a_sum[rb] = add[:HROW]
            b_sum[:, rb * BLK : (rb + 1) * BLK] = add[HROW:]

    def find_angles():
        run, across = at_lane, jnp.ones((1, TOK_SEQ), jnp.int32)
        for i in range(2 * N_TP):
            k = 2 * N_TP * s + i
            first, width = table[2, k], table[1, k] // 2
            inside = (at_lane >= first) & (at_lane < first + (table[0, k] // 2) * width)
            run = jnp.where(inside, first, run)
            across = jnp.where(inside, width, across)
        inner = (at_lane - run).astype(F32)
        wide = across.astype(F32)
        line = jnp.floor((inner + 0.5) / wide)
        begin = run.astype(F32)
        stack = jnp.concatenate(
            [begin, begin + line, begin + (inner - line * wide), jnp.zeros((5, TOK_SEQ), F32)], axis=0
        )
        turned = jnp.transpose(stack)
        f = lax.rem(lax.broadcasted_iota(jnp.int32, (1, D), 1), D // 2)
        position = jnp.where(f < 16, turned[:, 0:1], jnp.where(f < 40, turned[:, 1:2], turned[:, 2:3]))
        angle = position * frequency[...]
        cosine[...] = jnp.cos(angle)
        lane = lax.broadcasted_iota(jnp.int32, (1, D), 1)
        sine[...] = jnp.sin(angle) * jnp.where(lane < D // 2, -1.0, 1.0)

    def lift(n):
        cols = pl.ds(al(wrap(x + ORDER[n]) * VW, 128), VW)
        got = lax.dot_general(
            tokens[:, cols], up[:, cols], (((1,), (1,)), ((), ())), preferred_element_type=F32
        )
        if n == 0:
            lifted[...] = got + row_of(up_bias)
        else:
            lifted[...] += got

    def lift_first():
        load_up.wait()
        lift(0)
        for o in range(1, N_TP):
            frm = lax.rem(t - o + N_TP, N_TP)
            link.arrived(("o", o), o_cols.at[frm, o_place, :], frm)
        for sg, _ in SIGNS:
            along.send(("o", "z", sg), o_region(0, 0, None), o_region(0, 0, None), at(sg, 0))
        along.send(("o", "c", 0), o_region(0, 0, None), o_region(0, 0, None), at(0, 1))
        find_rows()

    def lift_second():
        lift(1)
        find_angles()

    def lift_third():
        lift(2)
        find_words()

    all_gather_2d(
        link, token_region, "t", None, (lift_first, lift_second, lift_third, functools.partial(lift, 3)), 1
    )

    raised = lifted[...]
    act = (0.5 * raised * (1.0 + lax.erf(raised * 0.5**0.5))).astype(BF16)
    hidden[...] = jnp.dot(pick_ref[...], act, preferred_element_type=F32).astype(BF16)
    load_down.wait()
    def lower_a(i):
        cols = pl.ds(al(wrap(x + i) * BLK, 128), BLK)
        got = jnp.dot(hidden[0:256, :], down[:, cols], preferred_element_type=F32)
        pa[:, :, cols] = got.astype(BF16).reshape(SIDE, HROW, BLK)

    def a_piece(i, part):
        rows = (pl.ds(0, SIDE), pl.ds(0, 2), pl.ds(2, 2))[0 if part is None else 1 + part]
        return pa.at[rows, :, pl.ds(al(wrap(x + i) * BLK, 128), BLK)]

    def b_piece(i, part):
        cols = (pl.ds(0, WIDTH), pl.ds(0, WIDTH // 2), pl.ds(WIDTH // 2, WIDTH // 2))[0 if part is None else 1 + part]
        return pb.at[wrap(y + i), :, cols]

    def to_x(sg):
        return at_xy(x + sg, y)

    def to_y(sg):
        return at_xy(x, y + sg)

    def mid_of(ref, name, part):
        if name == "a":
            return ref.at[pl.ds(2 * part, 2)]
        return ref.at[:, pl.ds(part * (WIDTH // 2), WIDTH // 2)]

    def make_a(i):
        lower_a(i)
        if i == 0:
            pa[:, :, own] = (pa[:, :, own].astype(F32) + a_sum[...].astype(F32)).astype(BF16)

    def make_b():
        for c in range(SIDE):
            cols = slice(c * BLK, (c + 1) * BLK)
            got = jnp.dot(hidden[256:, :], down[:, cols], preferred_element_type=F32)
            pb[:, :, cols] = got.astype(BF16).reshape(SIDE, HROW, BLK)
        for rb in range(SIDE):
            add = b_sum[:, rb * BLK : (rb + 1) * BLK].astype(F32)
            pb[rb, :, own] = (pb[rb, :, own].astype(F32) + add).astype(BF16)

    sides = (("a", a_piece, a_raw, a_mid, a_out, to_x), ("b", b_piece, b_raw, b_mid, b_out, to_y))

    def send_raw(n, piece, raw, mid, outb, to):
        for sg, part in SIGNS:
            link.send((n, "raw", sg), piece(2, part), raw.at[part], to(sg))

    def send_own(sg, part, n, piece, raw, mid, outb, to):
        link.send((n, "own", sg), piece(sg, 1 - part), mid_of(mid.at[part], n, 1 - part), to(sg))

    make_a(2)
    send_raw(*sides[0])
    make_b()
    send_raw(*sides[1])
    for sg, part in SIGNS:
        send_own(sg, part, *sides[1])
    for sg, part in SIGNS:
        make_a(sg)
        send_own(sg, part, *sides[0])
    for n, piece, raw, mid, outb, to in sides:
        for sg, part in SIGNS:
            link.arrived((n, "raw", sg), raw.at[part], to(-sg))
            outb[part] = (raw[part].astype(F32) + piece(sg, part)[...].astype(F32)).astype(BF16)
            link.send((n, "sum", sg), outb.at[part], mid_of(mid.at[part], n, part), to(sg))
    make_a(0)

    for sg, part in SIGNS:
        along.arrived(("o", "z", sg), o_region(-sg, 0, None), at(-sg, 0))
        along.send(("o", "r", sg), o_region(-sg, 0, part), o_region(-sg, 0, part), at(sg, 0))
        along.send(("o", "c", -sg), o_region(-sg, 0, None), o_region(-sg, 0, None), at(0, 1))

    def a_next(i):
        return a_sum.at[wrap(y + i)]

    def b_next(i):
        return b_sum.at[:, pl.ds(al(wrap(x + i) * BLK, 128), BLK)]

    after = ((0, a_next, to_y), (1, b_next, to_x))
    for side, nxt in zip(sides, after):
        n, piece, raw, mid, outb, to = side
        for sg, part in SIGNS:
            link.arrived((n, "own", sg), mid_of(mid.at[part], n, 1 - part), to(-sg))
            link.arrived((n, "sum", sg), mid_of(mid.at[part], n, part), to(-sg))
        held = a_sum if n == "a" else b_sum
        held[...] = (piece(0, None)[...].astype(F32) + mid[0].astype(F32) + mid[1].astype(F32)).astype(BF16)
        n, piece, to = nxt
        for k, (step_to, slot) in enumerate(DIRECT):
            link.send((n, "direct", k), piece(step_to), c_mid.at[n, slot], to(step_to))
    row = s * TOK_SEQ + y * RB + lax.broadcasted_iota(jnp.int32, (RB, 1), 0)
    image = jnp.zeros((RB, 1), F32)
    for e in range(N_TP):
        image = jnp.where((row >= start[e]) & (row < start[e] + length[e]), 1.0, image)
    full_bias = row_of(down_bias)
    shift = image * chosen(x, [full_bias[:, k * BLK : (k + 1) * BLK] for k in range(SIDE)])
    for n, piece, to in after:
        for k, (step_to, slot) in enumerate(DIRECT):
            link.arrived((n, "direct", k), c_mid.at[n, slot], to(-step_to))
        held = piece(0)[...].astype(F32)
        for slot in range(3):
            held = held + c_mid[n, slot].astype(F32)
        shard[pl.ds(n * HROW, HROW), :] = (held + shift[n * HROW : (n + 1) * HROW]).astype(BF16)

    for sg, part in SIGNS:
        along.arrived(("o", "r", sg), o_region(2, 0, part), at(-sg, 0))
        along.send(("o", "c", 2, part), o_region(2, 0, part), o_region(2, 0, part), at(0, 1))

    def region(half, x, y, part):
        first, count = ((0, HROW), (0, QROW), (QROW, QROW))[0 if part is None else 1 + part]
        return rows_ref.at[
            pl.ds(al(y * RB + half * HROW + first, QROW), count),
            pl.ds(al(x * BLK, 128), BLK),
        ]

    def kv_at(n, dz, dc):
        return kv.at[at(dz, dc), pl.ds(al(wrap(y + ORDER[n]) * RB, RB), RB), :]

    kv_row = row_of(kv_bias)
    heads_of = [kv_row[:, k * D : (k + 1) * D] for k in range(2 * KEY_VALUE_HEADS)]
    key_bias, value_bias = chosen(x, heads_of[:KEY_VALUE_HEADS]), chosen(x, heads_of[KEY_VALUE_HEADS:])

    def project(n):
        rows = pl.ds(al(wrap(y + ORDER[n]) * RB, RB), RB)
        value = rows_ref[rows, :].astype(F32)
        scale = lax.rsqrt(jnp.mean(value * value, axis=-1, keepdims=True) + EPS)
        normed[...] = (value * scale * row_of(gain)).astype(BF16)
        got = jnp.dot(normed[...], weight[...], preferred_element_type=F32)
        c, sn = cosine[rows, :], sine[rows, :]
        q, k = got[:, :D] + row_of(q_bias), got[:, D : 2 * D] + key_bias
        kv[s, rows, 0:D] = (k * c + pltpu.roll(k, D // 2, 1) * sn).astype(BF16)
        kv[s, rows, D : 2 * D] = (got[:, 2 * D :] + value_bias).astype(BF16)
        for sg, _ in SIGNS:
            along.send((n, "z", sg), kv_at(n, 0, 0), kv_at(n, 0, 0), at(sg, 0))
        along.send((n, "z", 2), kv_at(n, 0, 0), kv_at(n, 0, 0), at(2, 0))
        along.send((n, "c", 0), kv_at(n, 0, 0), kv_at(n, 0, 0), at(0, 1))
        query[rows, :] = (q * c + pltpu.roll(q, D // 2, 1) * sn).astype(BF16)

    def relay(n, steps):
        for dz in steps:
            along.arrived((n, "z", -dz if dz != 2 else 2), kv_at(n, dz, 0), at(dz, 0))
            along.send((n, "c", dz), kv_at(n, dz, 0), kv_at(n, dz, 0), at(0, 1))

    def first():
        for copy in load_qkv:
            copy.wait()
        project(0)

    def third():
        project(2)
        relay(0, (-1, 1, 2))

    def fourth():
        relay(1, (-1, 1, 2))
        project(3)
        relay(2, (-1, 1, 2))

    rows_ref[pl.ds(al(y * RB, RB), RB), own] = shard[...]
    all_gather_2d(
        link, region, "x", lambda half: shard.at[pl.ds(half * HROW, HROW)],
        (first, functools.partial(project, 1), third, fourth),
    )

    step = HEAD_DIMENSION ** (-0.5)
    chunk = 256

    def attend(b, causal):
        keys, values = kv[b, :, 0:D], kv[b, :, D : 2 * D]
        for r in range(TOK_SEQ // chunk):
            rows = slice(r * chunk, (r + 1) * chunk)
            width = (r + 1) * chunk if causal else TOK_SEQ
            score = lax.dot_general(query[rows, :], keys[:width], (((1,), (1,)), ((), ())), preferred_element_type=F32)
            if causal:
                down_row = lax.broadcasted_iota(jnp.int32, score.shape, 0) + r * chunk
                col = lax.broadcasted_iota(jnp.int32, score.shape, 1)
                score = jnp.where(col <= down_row, score, -1e30)
                top = jnp.max(score, axis=1, keepdims=True)
                p = jnp.exp((score - top) * step)
                total[rows, :] = jnp.sum(p, axis=1, keepdims=True)
                acc[rows, :] = jnp.dot(p.astype(BF16), values[:width], preferred_element_type=F32)
            else:
                old = best[rows, :]
                top = jnp.maximum(old, jnp.max(score, axis=1, keepdims=True))
                fade = jnp.exp((old - top) * step)
                p = jnp.exp((score - top) * step)
                total[rows, :] = total[rows, :] * fade + jnp.sum(p, axis=1, keepdims=True)
                acc[rows, :] = acc[rows, :] * fade + jnp.dot(p.astype(BF16), values, preferred_element_type=F32)
            best[rows, :] = top

    def attend_if(dz, dc):
        b = at(dz, dc)

        @pl.when(b < s)
        def _():
            attend(b, False)

    attend(s, True)
    relay(3, (-1, 1))
    for n in range(4):
        along.arrived((n, "c", 0), kv_at(n, 0, 1), at(0, 1))
    attend_if(0, 1)
    relay(3, (2,))
    for dz in (-1, 1, 2):
        attend_if(dz, 0)
        for n in range(4):
            along.arrived((n, "c", dz), kv_at(n, dz, 1), at(0, 1))
        attend_if(dz, 1)
    heads[:, pl.ds(al(t * D, 128), D)] = (acc[...] / total[...]).astype(BF16)

    def head_region(half, x, y, part):
        first, count = ((0, 256), (0, 128), (128, 128))[0 if part is None else 1 + part]
        return heads.at[pl.ds(half * 256 + first, count), pl.ds(al((x * SIDE + y) * D, 128), D)]

    def mix(n):
        if n == 0:
            for dz in (0, -1, 1):
                along.arrived(("o", "c", dz), o_region(dz, 1, None), at(0, 1))
            for part in (0, 1):
                along.arrived(("o", "c", 2, part), o_region(2, 1, part), at(0, 1))
            out_turned[...] = jnp.transpose(o_cols[...].reshape(LOCAL_QUERY_HEAD * D, COLS))
            out_sum[...] = lax.dot_general(
                spot, rows_ref[:, own], (((1,), (1,)), ((), ())), preferred_element_type=F32
            )
        cols = pl.ds(al(wrap(x + ORDER[n]) * SIDE * D, 128), SIDE * D)
        got = lax.dot_general(
            out_turned[:, cols], heads[:, cols], (((1,), (1,)), ((), ())), preferred_element_type=F32
        )
        if n < 3:
            out_sum[...] += got
        else:
            out[...] = (out_sum[...] + got).astype(BF16)

    all_gather_2d(link, head_region, "h", None, [functools.partial(mix, n) for n in range(4)], 1)
    link.drain()
    along.drain()


LINKS = 3 * AG_SEMS + 30 + 18
ALONG = 9 + 28


def run(*operands):
    vmem = pl.BlockSpec(memory_space=pltpu.VMEM)
    hbm = pl.BlockSpec(memory_space=pl.ANY)
    smem = pl.BlockSpec(memory_space=pltpu.SMEM)

    def b16(*shape):
        return pltpu.VMEM(shape, BF16)

    def f32(*shape):
        return pltpu.VMEM(shape, F32)

    return pl.pallas_call(
        body,
        out_shape=jax.ShapeDtypeStruct((COLS, TOK_SEQ), BF16),
        in_specs=[
            smem, hbm, vmem, vmem, hbm, vmem, hbm, vmem, hbm, vmem, hbm, vmem, hbm, vmem, hbm, vmem
        ],
        out_specs=vmem,
        scratch_shapes=[
            b16(HID, MW), b16(HID, WIDTH), b16(16, WIDTH), b16(N_TP, 16, COLS), b16(N_TP, D, COLS),
            b16(N_TP, 32, TCOL), b16(N_TP, 32, TCOL), b16(ROWS, MW), f32(ROWS, HID), b16(TOK_SEQ, HID),
            b16(SIDE, HROW, WIDTH), b16(SIDE, HROW, WIDTH),
            b16(2, 2, HROW, BLK), b16(2, SIDE, HROW, BLK), b16(2, 2, HROW, BLK), b16(SIDE, HROW, BLK),
            b16(2, HROW, WIDTH // 2), b16(2, HROW, WIDTH), b16(2, HROW, WIDTH // 2), b16(HROW, WIDTH),
            b16(2, 3, HROW, BLK), b16(RB, BLK),
            b16(TOK_SEQ, WIDTH), b16(WIDTH, 3 * D), b16(RB, WIDTH), b16(TOK_SEQ, D), b16(N_SEQ, TOK_SEQ, 2 * D),
            b16(TOK_SEQ, LOCAL_QUERY_HEAD * D), f32(TOK_SEQ, 1), f32(TOK_SEQ, 1), f32(TOK_SEQ, D),
            b16(TOK_SEQ, ROWS), f32(TOK_SEQ, D), f32(TOK_SEQ, D), b16(COLS, LOCAL_QUERY_HEAD * D), f32(COLS, TOK_SEQ),
            b16(4 * CAP, VW), b16(COLS, TOK_SEQ),
            pltpu.SemaphoreType.DMA((8,)),
            pltpu.SemaphoreType.DMA((LINKS,)), pltpu.SemaphoreType.DMA((LINKS,)),
            pltpu.SemaphoreType.DMA((ALONG,)), pltpu.SemaphoreType.DMA((ALONG,)),
        ],
        compiler_params=pltpu.CompilerParams(
            collective_id=0, has_side_effects=True, vmem_limit_bytes=60 * 1024 * 1024
        ),
        name="block",
    )(*operands)


def per_device(
    patches, image_table, ln_gain, ln_bias, merge_up, merge_up_bias, merge_down, merge_down_bias,
    text_embeds, attn_gain, q_weight, q_bias, key_value_weight, key_value_bias, o_weight,
):
    half = D // 2
    powers = np.float32(THETA) ** (np.float32(-2.0) * np.arange(half, dtype=np.float32) / np.float32(D))
    frequency = jnp.asarray(np.concatenate([powers, powers]).astype(np.float32).reshape(1, D))
    return run(
        image_table.T, patches, ln_gain, ln_bias, merge_up.T, merge_up_bias, merge_down, merge_down_bias,
        text_embeds.T, attn_gain, q_weight, q_bias, key_value_weight, key_value_bias, o_weight, frequency,
    ).T


def solution(mesh):
    return jax.shard_map(
        per_device,
        mesh=mesh,
        in_specs=(
            P(("seq", "tp"), None),
            P(),
            P(),
            P(),
            P(None, "tp"),
            P("tp"),
            P("tp", None),
            P(),
            P("seq", "tp"),
            P(),
            P(None, "tp"),
            P("tp"),
            P(),
            P(),
            P("tp", None),
        ),
        out_specs=P("seq", "tp"),
        check_vma=False,
    )
```

```python
import functools

import jax
import jax.numpy as jnp
import numpy as np
from jax import lax
from jax.experimental import pallas as pl
from jax.experimental.pallas import tpu as pltpu
from jax.sharding import PartitionSpec as P

MESH = pl.DeviceIdType.MESH
HEAD_DIMENSION = 128
KEY_VALUE_HEADS = 4
LOCAL_QUERY_HEAD = 16
CAP = 64
TOK_SEQ = 512
MW = 5120
VW = 1280
WIDTH = 3584
HID = 320
COLS = 224
N_TP = 16
N_SEQ = 8
SIDE = 4
ROWS = 448
HALF = 112
TCOL = 640
BLK = 896
RB = 128

EPS = 1e-06
THETA = 1000000.0
F32 = jnp.float32
BF16 = jnp.bfloat16


def al(value, multiple):
    return pl.multiple_of(value, multiple)


def place():
    t = lax.axis_index("tp")
    return t, t // SIDE, lax.rem(t, SIDE)


def wrap(value):
    return lax.rem(value + 2 * SIDE, SIDE)


def at_xy(x, y):
    return wrap(x) * SIDE + wrap(y)


def offset_xy(half, i, j):
    t, x, y = place()
    return (wrap(x + j), wrap(y + i)) if half == 0 else (wrap(x + i), wrap(y + j))


def peer(half, phase, sign):
    x, y = offset_xy(half, sign, 0) if phase == 1 else offset_xy(half, 0, sign)
    return x * SIDE + y


class Link:
    def __init__(self, send_sem, recv_sem, axis="tp"):
        self.send_sem, self.recv_sem, self.axis = send_sem, recv_sem, axis
        self.number, self.open = {}, []

    def _copy(self, key, src, dst, device):
        k = self.number.setdefault(key, len(self.number))
        return pltpu.make_async_remote_copy(
            src_ref=src,
            dst_ref=dst,
            send_sem=self.send_sem.at[k],
            recv_sem=self.recv_sem.at[k],
            device_id={self.axis: device},
            device_id_type=MESH,
        )

    def send(self, key, src, dst, device):
        copy = self._copy(key, src, dst, device)
        copy.start()
        self.open.append(copy)

    def arrived(self, key, dst, device):
        self._copy(key, dst, dst, device).wait_recv()

    def drain(self):
        assert len(self.number) <= self.send_sem.shape[0]
        for copy in self.open:
            copy.wait_send()
        self.open = []


def all_gather_2d(link, region, tag, own=None, hooks=(), lead=0):
    def reg(half, i, j, part):
        x, y = offset_xy(half, i, j)
        return region(half, x, y, part)

    def send(key, half, phase, sign, i, j, part):
        ref = reg(half, i, j, part)
        src = own(half) if own is not None and i == 0 and j == 0 else ref
        link.send((tag, half, *key), src, ref, peer(half, phase, sign))

    def got(key, half, phase, sign, i, j, part):
        link.arrived((tag, half, *key), reg(half, i, j, part), peer(half, phase, -sign))

    both = ((1, 0), (-1, 1))
    halves = (0, 1)

    def last(i, h):
        for s, part in both:
            got(("r2", s, i), h, 2, s, i, 2, part)

    for h in halves:
        for s, _ in both:
            send(("p1", s), h, 1, s, 0, 0, None)
    for h in halves:
        for s, _ in both:
            send(("p2", s, 0), h, 2, s, 0, 0, None)
    for s, part in both:
        for h in halves:
            got(("p1", s), h, 1, s, -s, 0, None)
            send(("r1", s), h, 1, s, -s, 0, part)
            for s2, _ in both:
                send(("p2", s2, -s), h, 2, s2, -s, 0, None)
    for s, part in both:
        for h in halves:
            got(("p2", s, 0), h, 2, s, 0, -s, None)
            send(("r2", s, 0), h, 2, s, 0, -s, part)
    for s, part in both:
        for h in halves:
            got(("r1", s), h, 1, s, 2, 0, part)
            for s2, _ in both:
                send(("p2", s2, 2, part), h, 2, s2, 2, 0, part)
    for i in (-1, 1):
        for s, part in both:
            for h in halves:
                got(("p2", s, i), h, 2, s, i, -s, None)
                send(("r2", s, i), h, 2, s, i, -s, part)
    last(0, lead)
    if hooks:
        hooks[0]()
    for s, part in both:
        for h in halves:
            got(("p2", s, 2, part), h, 2, s, 2, -s, part)
            send(("r2", s, 2), h, 2, s, 2, -s, part)
    for s, part in both:
        for h in halves:
            got(("p2", s, 2, 1 - part), h, 2, s, 2, -s, 1 - part)
    for n, i in enumerate((-1, 1)):
        last(i, lead)
        if hooks:
            hooks[1 + n]()
    last(2, lead)
    for i in (0, -1, 1, 2):
        last(i, 1 - lead)
    if hooks:
        hooks[3]()


AG_SEMS = 44


ORDER = (0, -1, 1, 2)
SIGNS = ((1, 0), (-1, 1))
DIRECT = ((2, 2), (1, 0), (-1, 1))
HROW = RB // 2
QROW = RB // 4
D = HEAD_DIMENSION


def chosen(index, pieces):
    value = pieces[0]
    for k in range(1, len(pieces)):
        value = jnp.where(index == k, pieces[k], value)
    return value


def row_of(ref):
    return ref[...].reshape(1, ref.shape[0])


def layout(table, s):
    start, length, base = [], [], []
    so_far = 0
    for e in range(N_TP):
        i = 2 * N_TP * s + 2 * e
        first = (table[0, i] // 2) * (table[1, i] // 2)
        second = (table[0, i + 1] // 2) * (table[1, i + 1] // 2)
        start.append(table[2, i])
        length.append(first + second)
        base.append(so_far)
        so_far = so_far + first + second
    return start, length, base


def body(
    table, patches_hbm, ln_gain, ln_bias, up_hbm, up_bias, down_hbm, down_bias, text_hbm, gain, q_weight, q_bias,
    kv_weight, kv_bias, o_hbm, frequency, out,
    up, down, o_rows, o_send, o_cols, outgoing, incoming, tokens, lifted, hidden, pa, pb,
    a_raw, a_mid, a_out, a_sum, b_raw, b_mid, b_out, b_sum, c_mid, shard,
    rows_ref, weight, normed, query, kv, heads, best, total, acc, pick_ref, cosine, sine, out_turned, out_sum, patches, text, load_sem, send_sem, recv_sem, seq_send, seq_recv,
):
    t, x, y = place()
    s = lax.axis_index("seq")
    z, core = s // 2, lax.rem(s, 2)

    def at(dz, dc):
        return lax.rem(z + dz + SIDE, SIDE) * 2 + lax.rem(core + dc, 2)

    barrier = pltpu.get_barrier_semaphore()
    for o in range(1, N_TP):
        pl.semaphore_signal(barrier, inc=1, device_id={"tp": lax.rem(t + o, N_TP)}, device_id_type=MESH)
    for device in (at(1, 0), at(-1, 0), at(0, 1)):
        pl.semaphore_signal(barrier, inc=1, device_id={"seq": device}, device_id_type=MESH)

    def load(n, src, dst):
        copy = pltpu.make_async_copy(src, dst, load_sem.at[n])
        copy.start()
        return copy

    load_patches = load(6, patches_hbm, patches)
    load_o = load(0, o_hbm.at[pl.ds(al(s * 16, 16), 16), :], o_rows)
    link = Link(send_sem, recv_sem)
    along = Link(seq_send, seq_recv, "seq")
    start, length, base = layout(table, s)

    load_patches.wait()
    value = patches[...].astype(F32)
    centre = jnp.mean(value, axis=-1, keepdims=True)
    centred = value - centre
    spread = jnp.mean(centred * centred, axis=-1, keepdims=True)
    fine = (centred * lax.rsqrt(spread + EPS) * row_of(ln_gain) + row_of(ln_bias)).astype(BF16)
    my_base, my_length = chosen(t, base), chosen(t, length)
    slot = lax.broadcasted_iota(jnp.int32, (CAP, 4 * CAP), 0)
    lane = lax.broadcasted_iota(jnp.int32, (CAP, 4 * CAP), 1)
    token = 2 * lax.rem(slot, 32) + lax.rem(slot // 32 + my_base, 2)
    source = jnp.where(token < my_length, 4 * token, -8)
    for i in (1, 2, 3, 0):
        q = wrap(x + i)
        part = jnp.dot((lane == source + q).astype(BF16), fine, preferred_element_type=F32).astype(BF16)
        for u in range(2):
            for r in range(2):
                outgoing[4 * q + 2 * u + r] = part[r * 32 : (r + 1) * 32, u * TCOL : (u + 1) * TCOL]
    pl.semaphore_wait(barrier, N_TP + 2)
    for i in (1, 2, 3, 0):
        for j in (1, 2, 3, 0):
            k = (i + j) % SIDE
            if (k, j) != (0, 0):
                to = at_xy(x + k, y + j)
                link.send(("a", k, j), outgoing.at[to], incoming.at[t], to)
    incoming[t] = outgoing[t]

    load_o.wait()
    o_all = o_rows[...]
    for d in range(N_TP):
        o_send[d] = o_all[:, d * COLS : (d + 1) * COLS]
    o_place = pl.ds(al(s * 16, 16), 16)
    for o in range(1, N_TP):
        to = lax.rem(t + o, N_TP)
        link.send(("o", o), o_send.at[to], o_cols.at[t, o_place, :], to)
    o_cols[t, o_place, :] = o_send[t]

    load_up = load(1, up_hbm, up)
    load_down = load(2, down_hbm, down)
    load_text = load(7, text_hbm, text)
    load_qkv = [
        load(3, q_weight, weight.at[:, pl.ds(0, D)]),
        load(4, kv_weight.at[:, pl.ds(al(x * D, 128), D)], weight.at[:, pl.ds(D, D)]),
        load(5, kv_weight.at[:, pl.ds(al((KEY_VALUE_HEADS + x) * D, 128), D)], weight.at[:, pl.ds(2 * D, D)]),
    ]

    half_of = lax.rem(t, 2)
    lane = lax.broadcasted_iota(jnp.int32, (1, N_TP * 32), 1)
    base_row = jnp.zeros((1, N_TP * 32), jnp.int32)
    length_row = base_row
    for e in range(N_TP):
        here = lane // 32 == e
        base_row = jnp.where(here, base[e], base_row)
        length_row = jnp.where(here, length[e], length_row)
    taken = 2 * lax.rem(lane, 32) + lax.rem(half_of + base_row, 2)
    target = jnp.where(taken < length_row, (base_row + taken) // 2, -1)
    pick = (lax.broadcasted_iota(jnp.int32, (2 * HALF, N_TP * 32), 0) == target).astype(BF16)
    for i in (1, 2, 3, 0):
        for j in (1, 2, 3, 0):
            if (i, j) != (0, 0):
                frm = at_xy(x - i, y - j)
                link.arrived(("a", i, j), incoming.at[frm], frm)
    slots = incoming[...].reshape(N_TP * 32, TCOL)
    mine = jnp.dot(pick, slots, preferred_element_type=F32).astype(BF16)
    tokens[pl.ds(al(half_of * 2 * HALF, 2 * HALF), 2 * HALF), pl.ds(al(t // 2 * TCOL, 128), TCOL)] = mine

    def token_region(half, x, y, part):
        d = x * SIDE + y
        first, width = ((0, TCOL), (0, 384), (384, 256))[0 if part is None else 1 + part]
        return tokens.at[
            pl.ds(al(lax.rem(d, 2) * 2 * HALF + half * HALF, 16), HALF),
            pl.ds(al(d // 2 * TCOL + first, 128), width),
        ]

    def o_region(dz, dc, part):
        first, count = ((0, N_TP), (0, 8), (8, 8))[0 if part is None else 1 + part]
        return o_cols.at[pl.ds(first, count), pl.ds(al(at(dz, dc) * 16, 16), 16), :]

    spot = (
        lax.broadcasted_iota(jnp.int32, (COLS, BLK), 0) + y * COLS == lax.broadcasted_iota(jnp.int32, (COLS, BLK), 1)
    ).astype(BF16)
    own = pl.ds(al(x * BLK, 128), BLK)
    at_lane = s * TOK_SEQ + lax.broadcasted_iota(jnp.int32, (1, TOK_SEQ), 1)

    def find_rows():
        order = lax.broadcasted_iota(jnp.int32, (TOK_SEQ, 1), 0)
        pos = s * TOK_SEQ + lax.rem(order, 256) // HROW * RB + order // 256 * HROW + lax.rem(order, HROW)
        where = jnp.full((TOK_SEQ, 1), -1, jnp.int32)
        for e in range(N_TP):
            inner = pos - start[e]
            where = jnp.where((inner >= 0) & (inner < length[e]), base[e] + inner, where)
        where = jnp.where(where >= 0, lax.rem(where, 2) * 2 * HALF + where // 2, -1)
        pick_ref[...] = (lax.broadcasted_iota(jnp.int32, (TOK_SEQ, ROWS), 1) == where).astype(BF16)

    def find_words():
        load_text.wait()
        plain = jnp.ones((1, TOK_SEQ), F32)
        for e in range(N_TP):
            plain = jnp.where((at_lane >= start[e]) & (at_lane < start[e] + length[e]), 0.0, plain)
        words = (text[...].astype(F32) * plain).astype(BF16)
        for rb in range(SIDE):
            add = lax.dot_general(
                words[:, rb * RB : (rb + 1) * RB], spot, (((0,), (0,)), ((), ())), preferred_element_type=F32
            ).astype(BF16)
            a_sum[rb] = add[:HROW]
            b_sum[:, rb * BLK : (rb + 1) * BLK] = add[HROW:]

    def find_angles():
        run, across = at_lane, jnp.ones((1, TOK_SEQ), jnp.int32)
        for i in range(2 * N_TP):
            k = 2 * N_TP * s + i
            first, width = table[2, k], table[1, k] // 2
            inside = (at_lane >= first) & (at_lane < first + (table[0, k] // 2) * width)
            run = jnp.where(inside, first, run)
            across = jnp.where(inside, width, across)
        inner = (at_lane - run).astype(F32)
        wide = across.astype(F32)
        line = jnp.floor((inner + 0.5) / wide)
        begin = run.astype(F32)
        stack = jnp.concatenate(
            [begin, begin + line, begin + (inner - line * wide), jnp.zeros((5, TOK_SEQ), F32)], axis=0
        )
        turned = jnp.transpose(stack)
        f = lax.rem(lax.broadcasted_iota(jnp.int32, (1, D), 1), D // 2)
        position = jnp.where(f < 16, turned[:, 0:1], jnp.where(f < 40, turned[:, 1:2], turned[:, 2:3]))
        angle = position * frequency[...]
        cosine[...] = jnp.cos(angle)
        lane = lax.broadcasted_iota(jnp.int32, (1, D), 1)
        sine[...] = jnp.sin(angle) * jnp.where(lane < D // 2, -1.0, 1.0)

    def lift(n):
        cols = pl.ds(al(wrap(x + ORDER[n]) * VW, 128), VW)
        got = lax.dot_general(
            tokens[:, cols], up[:, cols], (((1,), (1,)), ((), ())), preferred_element_type=F32
        )
        if n == 0:
            lifted[...] = got + row_of(up_bias)
        else:
            lifted[...] += got

    def lift_first():
        load_up.wait()
        lift(0)
        for o in range(1, N_TP):
            frm = lax.rem(t - o + N_TP, N_TP)
            link.arrived(("o", o), o_cols.at[frm, o_place, :], frm)
        for sg, _ in SIGNS:
            along.send(("o", "z", sg), o_region(0, 0, None), o_region(0, 0, None), at(sg, 0))
        along.send(("o", "c", 0), o_region(0, 0, None), o_region(0, 0, None), at(0, 1))
        find_rows()

    def lift_second():
        lift(1)
        find_angles()

    def lift_third():
        lift(2)
        find_words()

    all_gather_2d(
        link, token_region, "t", None, (lift_first, lift_second, lift_third, functools.partial(lift, 3)), 1
    )

    raised = lifted[...]
    act = (0.5 * raised * (1.0 + lax.erf(raised * 0.5**0.5))).astype(BF16)
    hidden[...] = jnp.dot(pick_ref[...], act, preferred_element_type=F32).astype(BF16)
    load_down.wait()
    def lower_a(i):
        cols = pl.ds(al(wrap(x + i) * BLK, 128), BLK)
        got = jnp.dot(hidden[0:256, :], down[:, cols], preferred_element_type=F32)
        pa[:, :, cols] = got.astype(BF16).reshape(SIDE, HROW, BLK)

    def a_piece(i, part):
        rows = (pl.ds(0, SIDE), pl.ds(0, 2), pl.ds(2, 2))[0 if part is None else 1 + part]
        return pa.at[rows, :, pl.ds(al(wrap(x + i) * BLK, 128), BLK)]

    def b_piece(i, part):
        cols = (pl.ds(0, WIDTH), pl.ds(0, WIDTH // 2), pl.ds(WIDTH // 2, WIDTH // 2))[0 if part is None else 1 + part]
        return pb.at[wrap(y + i), :, cols]

    def to_x(sg):
        return at_xy(x + sg, y)

    def to_y(sg):
        return at_xy(x, y + sg)

    def mid_of(ref, name, part):
        if name == "a":
            return ref.at[pl.ds(2 * part, 2)]
        return ref.at[:, pl.ds(part * (WIDTH // 2), WIDTH // 2)]

    def make_a(i):
        lower_a(i)
        if i == 0:
            pa[:, :, own] = (pa[:, :, own].astype(F32) + a_sum[...].astype(F32)).astype(BF16)

    def make_b():
        for c in range(SIDE):
            cols = slice(c * BLK, (c + 1) * BLK)
            got = jnp.dot(hidden[256:, :], down[:, cols], preferred_element_type=F32)
            pb[:, :, cols] = got.astype(BF16).reshape(SIDE, HROW, BLK)
        for rb in range(SIDE):
            add = b_sum[:, rb * BLK : (rb + 1) * BLK].astype(F32)
            pb[rb, :, own] = (pb[rb, :, own].astype(F32) + add).astype(BF16)

    sides = (("a", a_piece, a_raw, a_mid, a_out, to_x), ("b", b_piece, b_raw, b_mid, b_out, to_y))

    def send_raw(n, piece, raw, mid, outb, to):
        for sg, part in SIGNS:
            link.send((n, "raw", sg), piece(2, part), raw.at[part], to(sg))

    def send_own(sg, part, n, piece, raw, mid, outb, to):
        link.send((n, "own", sg), piece(sg, 1 - part), mid_of(mid.at[part], n, 1 - part), to(sg))

    make_a(2)
    send_raw(*sides[0])
    make_b()
    send_raw(*sides[1])
    for sg, part in SIGNS:
        send_own(sg, part, *sides[1])
    for sg, part in SIGNS:
        make_a(sg)
        send_own(sg, part, *sides[0])
    for n, piece, raw, mid, outb, to in sides:
        for sg, part in SIGNS:
            link.arrived((n, "raw", sg), raw.at[part], to(-sg))
            outb[part] = (raw[part].astype(F32) + piece(sg, part)[...].astype(F32)).astype(BF16)
            link.send((n, "sum", sg), outb.at[part], mid_of(mid.at[part], n, part), to(sg))
    make_a(0)

    for sg, part in SIGNS:
        along.arrived(("o", "z", sg), o_region(-sg, 0, None), at(-sg, 0))
        along.send(("o", "r", sg), o_region(-sg, 0, part), o_region(-sg, 0, part), at(sg, 0))
        along.send(("o", "c", -sg), o_region(-sg, 0, None), o_region(-sg, 0, None), at(0, 1))

    def a_next(i):
        return a_sum.at[wrap(y + i)]

    def b_next(i):
        return b_sum.at[:, pl.ds(al(wrap(x + i) * BLK, 128), BLK)]

    after = ((0, a_next, to_y), (1, b_next, to_x))
    for side, nxt in zip(sides, after):
        n, piece, raw, mid, outb, to = side
        for sg, part in SIGNS:
            link.arrived((n, "own", sg), mid_of(mid.at[part], n, 1 - part), to(-sg))
            link.arrived((n, "sum", sg), mid_of(mid.at[part], n, part), to(-sg))
        held = a_sum if n == "a" else b_sum
        held[...] = (piece(0, None)[...].astype(F32) + mid[0].astype(F32) + mid[1].astype(F32)).astype(BF16)
        n, piece, to = nxt
        for k, (step_to, slot) in enumerate(DIRECT):
            link.send((n, "direct", k), piece(step_to), c_mid.at[n, slot], to(step_to))
    row = s * TOK_SEQ + y * RB + lax.broadcasted_iota(jnp.int32, (RB, 1), 0)
    image = jnp.zeros((RB, 1), F32)
    for e in range(N_TP):
        image = jnp.where((row >= start[e]) & (row < start[e] + length[e]), 1.0, image)
    full_bias = row_of(down_bias)
    shift = image * chosen(x, [full_bias[:, k * BLK : (k + 1) * BLK] for k in range(SIDE)])
    for n, piece, to in after:
        for k, (step_to, slot) in enumerate(DIRECT):
            link.arrived((n, "direct", k), c_mid.at[n, slot], to(-step_to))
        held = piece(0)[...].astype(F32)
        for slot in range(3):
            held = held + c_mid[n, slot].astype(F32)
        shard[pl.ds(n * HROW, HROW), :] = (held + shift[n * HROW : (n + 1) * HROW]).astype(BF16)

    for sg, part in SIGNS:
        along.arrived(("o", "r", sg), o_region(2, 0, part), at(-sg, 0))
        along.send(("o", "c", 2, part), o_region(2, 0, part), o_region(2, 0, part), at(0, 1))

    def region(half, x, y, part):
        first, count = ((0, HROW), (0, QROW), (QROW, QROW))[0 if part is None else 1 + part]
        return rows_ref.at[
            pl.ds(al(y * RB + half * HROW + first, QROW), count),
            pl.ds(al(x * BLK, 128), BLK),
        ]

    def kv_at(n, dz, dc):
        return kv.at[at(dz, dc), pl.ds(al(wrap(y + ORDER[n]) * RB, RB), RB), :]

    kv_row = row_of(kv_bias)
    heads_of = [kv_row[:, k * D : (k + 1) * D] for k in range(2 * KEY_VALUE_HEADS)]
    key_bias, value_bias = chosen(x, heads_of[:KEY_VALUE_HEADS]), chosen(x, heads_of[KEY_VALUE_HEADS:])

    def project(n):
        rows = pl.ds(al(wrap(y + ORDER[n]) * RB, RB), RB)
        value = rows_ref[rows, :].astype(F32)
        scale = lax.rsqrt(jnp.mean(value * value, axis=-1, keepdims=True) + EPS)
        normed[...] = (value * scale * row_of(gain)).astype(BF16)
        got = jnp.dot(normed[...], weight[...], preferred_element_type=F32)
        c, sn = cosine[rows, :], sine[rows, :]
        q, k = got[:, :D] + row_of(q_bias), got[:, D : 2 * D] + key_bias
        kv[s, rows, 0:D] = (k * c + pltpu.roll(k, D // 2, 1) * sn).astype(BF16)
        kv[s, rows, D : 2 * D] = (got[:, 2 * D :] + value_bias).astype(BF16)
        for sg, _ in SIGNS:
            along.send((n, "z", sg), kv_at(n, 0, 0), kv_at(n, 0, 0), at(sg, 0))
        along.send((n, "z", 2), kv_at(n, 0, 0), kv_at(n, 0, 0), at(2, 0))
        along.send((n, "c", 0), kv_at(n, 0, 0), kv_at(n, 0, 0), at(0, 1))
        query[rows, :] = (q * c + pltpu.roll(q, D // 2, 1) * sn).astype(BF16)

    def relay(n, steps):
        for dz in steps:
            along.arrived((n, "z", -dz if dz != 2 else 2), kv_at(n, dz, 0), at(dz, 0))
            along.send((n, "c", dz), kv_at(n, dz, 0), kv_at(n, dz, 0), at(0, 1))

    def first():
        for copy in load_qkv:
            copy.wait()
        project(0)

    def third():
        project(2)
        relay(0, (-1, 1, 2))

    def fourth():
        relay(1, (-1, 1, 2))
        project(3)
        relay(2, (-1, 1, 2))

    rows_ref[pl.ds(al(y * RB, RB), RB), own] = shard[...]
    all_gather_2d(
        link, region, "x", lambda half: shard.at[pl.ds(half * HROW, HROW)],
        (first, functools.partial(project, 1), third, fourth),
    )

    step = HEAD_DIMENSION ** (-0.5)
    chunk = 256

    def attend(b, causal):
        keys, values = kv[b, :, 0:D], kv[b, :, D : 2 * D]
        for r in range(TOK_SEQ // chunk):
            rows = slice(r * chunk, (r + 1) * chunk)
            width = (r + 1) * chunk if causal else TOK_SEQ
            score = lax.dot_general(query[rows, :], keys[:width], (((1,), (1,)), ((), ())), preferred_element_type=F32)
            if causal:
                down_row = lax.broadcasted_iota(jnp.int32, score.shape, 0) + r * chunk
                col = lax.broadcasted_iota(jnp.int32, score.shape, 1)
                score = jnp.where(col <= down_row, score, -1e30)
                top = jnp.max(score, axis=1, keepdims=True)
                p = jnp.exp((score - top) * step)
                total[rows, :] = jnp.sum(p, axis=1, keepdims=True)
                acc[rows, :] = jnp.dot(p.astype(BF16), values[:width], preferred_element_type=F32)
            else:
                old = best[rows, :]
                top = jnp.maximum(old, jnp.max(score, axis=1, keepdims=True))
                fade = jnp.exp((old - top) * step)
                p = jnp.exp((score - top) * step)
                total[rows, :] = total[rows, :] * fade + jnp.sum(p, axis=1, keepdims=True)
                acc[rows, :] = acc[rows, :] * fade + jnp.dot(p.astype(BF16), values, preferred_element_type=F32)
            best[rows, :] = top

    def attend_if(dz, dc):
        b = at(dz, dc)

        @pl.when(b < s)
        def _():
            attend(b, False)

    attend(s, True)
    relay(3, (-1, 1))
    for n in range(4):
        along.arrived((n, "c", 0), kv_at(n, 0, 1), at(0, 1))
    attend_if(0, 1)
    relay(3, (2,))
    for dz in (-1, 1, 2):
        attend_if(dz, 0)
        for n in range(4):
            along.arrived((n, "c", dz), kv_at(n, dz, 1), at(0, 1))
        attend_if(dz, 1)
    heads[:, pl.ds(al(t * D, 128), D)] = (acc[...] / total[...]).astype(BF16)

    def head_region(half, x, y, part):
        first, count = ((0, 256), (0, 128), (128, 128))[0 if part is None else 1 + part]
        return heads.at[pl.ds(half * 256 + first, count), pl.ds(al((x * SIDE + y) * D, 128), D)]

    def mix(n):
        if n == 0:
            for dz in (0, -1, 1):
                along.arrived(("o", "c", dz), o_region(dz, 1, None), at(0, 1))
            for part in (0, 1):
                along.arrived(("o", "c", 2, part), o_region(2, 1, part), at(0, 1))
            out_turned[...] = jnp.transpose(o_cols[...].reshape(LOCAL_QUERY_HEAD * D, COLS))
            out_sum[...] = lax.dot_general(
                spot, rows_ref[:, own], (((1,), (1,)), ((), ())), preferred_element_type=F32
            )
        cols = pl.ds(al(wrap(x + ORDER[n]) * SIDE * D, 128), SIDE * D)
        got = lax.dot_general(
            out_turned[:, cols], heads[:, cols], (((1,), (1,)), ((), ())), preferred_element_type=F32
        )
        if n < 3:
            out_sum[...] += got
        else:
            out[...] = (out_sum[...] + got).astype(BF16)

    all_gather_2d(link, head_region, "h", None, [functools.partial(mix, n) for n in range(4)], 1)
    link.drain()
    along.drain()


LINKS = 3 * AG_SEMS + 30 + 18
ALONG = 9 + 28


def run(*operands):
    vmem = pl.BlockSpec(memory_space=pltpu.VMEM)
    hbm = pl.BlockSpec(memory_space=pl.ANY)
    smem = pl.BlockSpec(memory_space=pltpu.SMEM)

    def b16(*shape):
        return pltpu.VMEM(shape, BF16)

    def f32(*shape):
        return pltpu.VMEM(shape, F32)

    return pl.pallas_call(
        body,
        out_shape=jax.ShapeDtypeStruct((COLS, TOK_SEQ), BF16),
        in_specs=[
            smem, hbm, vmem, vmem, hbm, vmem, hbm, vmem, hbm, vmem, hbm, vmem, hbm, vmem, hbm, vmem
        ],
        out_specs=vmem,
        scratch_shapes=[
            b16(HID, MW), b16(HID, WIDTH), b16(16, WIDTH), b16(N_TP, 16, COLS), b16(N_TP, D, COLS),
            b16(N_TP, 32, TCOL), b16(N_TP, 32, TCOL), b16(ROWS, MW), f32(ROWS, HID), b16(TOK_SEQ, HID),
            b16(SIDE, HROW, WIDTH), b16(SIDE, HROW, WIDTH),
            b16(2, 2, HROW, BLK), b16(2, SIDE, HROW, BLK), b16(2, 2, HROW, BLK), b16(SIDE, HROW, BLK),
            b16(2, HROW, WIDTH // 2), b16(2, HROW, WIDTH), b16(2, HROW, WIDTH // 2), b16(HROW, WIDTH),
            b16(2, 3, HROW, BLK), b16(RB, BLK),
            b16(TOK_SEQ, WIDTH), b16(WIDTH, 3 * D), b16(RB, WIDTH), b16(TOK_SEQ, D), b16(N_SEQ, TOK_SEQ, 2 * D),
            b16(TOK_SEQ, LOCAL_QUERY_HEAD * D), f32(TOK_SEQ, 1), f32(TOK_SEQ, 1), f32(TOK_SEQ, D),
            b16(TOK_SEQ, ROWS), f32(TOK_SEQ, D), f32(TOK_SEQ, D), b16(COLS, LOCAL_QUERY_HEAD * D), f32(COLS, TOK_SEQ),
            b16(4 * CAP, VW), b16(COLS, TOK_SEQ),
            pltpu.SemaphoreType.DMA((8,)),
            pltpu.SemaphoreType.DMA((LINKS,)), pltpu.SemaphoreType.DMA((LINKS,)),
            pltpu.SemaphoreType.DMA((ALONG,)), pltpu.SemaphoreType.DMA((ALONG,)),
        ],
        compiler_params=pltpu.CompilerParams(
            collective_id=0, has_side_effects=True, vmem_limit_bytes=60 * 1024 * 1024
        ),
        name="block",
    )(*operands)


def per_device(
    patches, image_table, ln_gain, ln_bias, merge_up, merge_up_bias, merge_down, merge_down_bias,
    text_embeds, attn_gain, q_weight, q_bias, key_value_weight, key_value_bias, o_weight,
):
    half = D // 2
    powers = np.float32(THETA) ** (np.float32(-2.0) * np.arange(half, dtype=np.float32) / np.float32(D))
    frequency = jnp.asarray(np.concatenate([powers, powers]).astype(np.float32).reshape(1, D))
    return run(
        image_table.T, patches, ln_gain, ln_bias, merge_up.T, merge_up_bias, merge_down, merge_down_bias,
        text_embeds.T, attn_gain, q_weight, q_bias, key_value_weight, key_value_bias, o_weight, frequency,
    ).T


def solution(mesh):
    return jax.shard_map(
        per_device,
        mesh=mesh,
        in_specs=(
            P(("seq", "tp"), None),
            P(),
            P(),
            P(),
            P(None, "tp"),
            P("tp"),
            P("tp", None),
            P(),
            P("seq", "tp"),
            P(),
            P(None, "tp"),
            P("tp"),
            P(),
            P(),
            P("tp", None),
        ),
        out_specs=P("seq", "tp"),
        check_vma=False,
    )
```
